32 devices in a mesh: freq: 2 (over y), rcv: 4 (over z), src: 4 (over x, core).
Axes of the slice: x: 2, y: 2, z: 4, core: 2. Of those that a mesh axis runs over, the one named last changes fastest.
Arguments:
- traces: float32 [256, 2, 4096], P(('freq', 'src'), None, 'rcv'), parts along dimension 0, may hold values from -6 to 6
- moveout: float32 [2, 64, 16], P(None, 'freq'), parts along dimension 1, may hold values from -0.75 to 0.75
- trace_owner: int32 [8192], P(('freq', 'rcv')), parts along dimension 0, may hold values from 0 to 3, as said below
- trace_group: int32 [8192], P(('freq', 'rcv')), parts along dimension 0, may hold values from 0 to 127
- trace_table: int32 [8192], P(('freq', 'rcv')), parts along dimension 0, may hold values from 0 to 31
- aperture: float32 [2, 16384, 8192], P(None, ('freq', 'rcv'), 'src'), parts along dimension 1, may hold values from -0.046875 to 0.046875
- shaping: float32 [256, 2, 8192], P(('freq', 'src'), None, 'rcv'), parts along dimension 0, may hold values from -0.5 to 0.5
Outputs:
- demultiple: float32 [256, 2, 8192], P(('freq', 'src'), None, 'rcv'), parts along dimension 0
The draws below stay inside these ranges and needn't reach their ends.
There are 2 independent parts, one for each index of `freq`. The reference program is written for one: setup_inputs(seed, part) draws one part's arguments, and reference() takes and returns one part's arrays. A program takes and returns all parts, laid end to end along the dimension named above; each array names one. Nothing has to cross between parts.
Inputs may be any that keep to these rules, and one draw needn't show every extreme that they name: `trace_owner`: among the 1024 traces of each index of rcv (aligned blocks of the array), at most 512 name the same owner, and in every draw some owner is named by exactly 512 traces of every block.
All inputs are finite; a program needn't handle non-finite values.
Results may differ from the reference program's by a relative error of at most 0.0001.
Values sent between devices are 32-bit elements; how exact they have to be, the bound alone decides.
A program may use at most 128 MiB of HBM per device.

```python
import jax
import jax.numpy as jnp
from jax import lax

BINS = 8192
STENCIL = 16
TABLES = 32
ITERS = 2
TRACE_DEV = 1024
SHOTS = 128
TRACES = 4096
GROUPS = 128
CAPACITY = 512
N_RCV = 4


def draw_trace_owner(key, part):
    slot_total = N_RCV * CAPACITY
    owner_of_slot = jnp.arange(slot_total, dtype=jnp.int32) // CAPACITY
    owner_bias = jax.random.randint(jax.random.fold_in(key, 11), (N_RCV,), 0, 4096)
    forced_owner = jax.random.randint(jax.random.fold_in(key, 12), (), 0, N_RCV)

    def one_device(device_index):
        device_key = jax.random.fold_in(jax.random.fold_in(key, 13), device_index)
        slot_noise = jax.random.randint(jax.random.fold_in(device_key, 1), (slot_total,), 0, 4096)
        slot_score = slot_noise + owner_bias[owner_of_slot]
        slot_score = jnp.where(owner_of_slot == forced_owner, -1, slot_score)
        slot_score = (slot_score + 1) * slot_total + jnp.arange(slot_total, dtype=jnp.int32)
        chosen = jnp.argsort(slot_score)[:TRACE_DEV]
        shuffle = jax.random.permutation(jax.random.fold_in(device_key, 2), TRACE_DEV)
        return owner_of_slot[chosen][shuffle]
    return jax.vmap(one_device)(jnp.arange(N_RCV, dtype=jnp.int32)).reshape(-1).astype(jnp.int32)


def place_ends(drawn, own_key, smallest, largest):
    longest = drawn.shape.index(max(drawn.shape))
    spots = []
    for shift in (0, 1):
        where = [jax.random.randint(jax.random.fold_in(own_key, axis), (), 0, length) for axis, length in enumerate(drawn.shape)]
        where[longest] = (where[longest] + shift) % drawn.shape[longest]
        spots.append(tuple(where))
    return drawn.at[spots[0]].set(smallest).at[spots[1]].set(largest)


def block_scale(stream_key, extent, shards, least, largest):
    gain, own = 1.0, jax.random.fold_in(stream_key, 6)
    for dim, blocks in shards:
        heights = jnp.exp(jax.random.uniform(jax.random.fold_in(own, dim), (blocks,), jnp.float32, least / len(shards), largest / len(shards)))
        gain = gain * jnp.repeat(heights, extent[dim] // blocks).reshape([-1 if axis == dim else 1 for axis in range(len(extent))])
    return gain


def gaussian(rng, extent, scale, reach, shards=(), kind=jnp.bfloat16):
    drawn = jax.random.normal(rng, extent, jnp.float32) * scale
    if len(shards) > 0:
        drawn = block_scale(rng, extent, shards, -0.22, 0.18) * drawn
    return jnp.clip(drawn, min=-reach, max=reach).astype(kind)


def setup_inputs(seed: int = 0, part: int = 0) -> dict:
    key_of = jax.random.split(jax.random.key(seed), 8)
    own_keys = jax.random.split(jax.random.fold_in(key_of[7], part), 8)
    return {
        "traces": gaussian(own_keys[0], (SHOTS, 2, TRACES), 1.0, 6.0, ((0, 4), (2, 4)), jnp.float32),
        "moveout": gaussian(own_keys[1], (2, TABLES, STENCIL), 0.125, 0.75, (), jnp.float32),
        "trace_owner": draw_trace_owner(jax.random.fold_in(jax.random.fold_in(key_of[7], part), 71), part),
        "trace_group": place_ends(jax.random.randint(own_keys[3], (TRACES,), 0, GROUPS), jax.random.fold_in(own_keys[3], 1), 0, GROUPS - 1).astype(jnp.int32),
        "trace_table": place_ends(jax.random.randint(own_keys[4], (TRACES,), 0, TABLES), jax.random.fold_in(own_keys[4], 1), 0, TABLES - 1).astype(jnp.int32),
        "aperture": gaussian(own_keys[5], (2, BINS, BINS), (2 * BINS) ** -0.5, 0.046875, ((1, 4), (2, 4)), jnp.float32),
        "shaping": jnp.clip(jax.random.uniform(own_keys[6], (SHOTS, 2, BINS), jnp.float32, -0.5, 0.5) * block_scale(own_keys[6], (SHOTS, 2, BINS), ((0, 4), (2, 4)), -0.4, 0.0), -0.5, 0.5),
    }


def complex_join(partial_terms):
    return jnp.stack([partial_terms[:, 0, 0] - partial_terms[:, 1, 1], partial_terms[:, 0, 1] + partial_terms[:, 1, 0]], axis=1)


def complex_product(left_side, right_side):
    real_part = left_side[:, 0] * right_side[:, 0] - left_side[:, 1] * right_side[:, 1]
    imag_part = left_side[:, 0] * right_side[:, 1] + left_side[:, 1] * right_side[:, 0]
    return jnp.stack([real_part, imag_part], axis=1)


def reference(traces, moveout, trace_owner, trace_group, trace_table, aperture, shaping):
    highest = lax.Precision.HIGHEST
    bin_block = (trace_owner * GROUPS + trace_group).astype(jnp.int32)
    weights = moveout[:, trace_table, :]
    values = jnp.transpose(traces, (2, 1, 0))
    real_part = values[:, 0, None, :] * weights[0][:, :, None] - values[:, 1, None, :] * weights[1][:, :, None]
    real_sum = jax.ops.segment_sum(real_part, bin_block, num_segments=BINS // STENCIL)
    imag_part = values[:, 0, None, :] * weights[1][:, :, None] + values[:, 1, None, :] * weights[0][:, :, None]
    imag_sum = jax.ops.segment_sum(imag_part, bin_block, num_segments=BINS // STENCIL)
    binned = jnp.stack([real_sum, imag_sum], 0).reshape(2, BINS, SHOTS).transpose(2, 0, 1)
    panel_now = binned
    for sweep_index in range(ITERS):
        multiples = complex_join(jnp.einsum("sck,dik->scdi", panel_now, aperture, precision=highest))
        panel_now = binned - complex_product(shaping, multiples)
    return panel_now
```

```python
import functools

import jax
import jax.numpy as jnp
from jax import lax
from jax.experimental import pallas as pl
from jax.experimental.pallas import tpu as pltpu
from jax.sharding import PartitionSpec as P

ITERS = 2
MESH = pl.DeviceIdType.MESH
F32 = jnp.float32
BF16 = jnp.bfloat16
NT = (((1,), (1,)), ((), ()))


def split(value):
    high = value.astype(BF16)
    return high, (value - high.astype(F32)).astype(BF16)


def remote(src, dst, send_sem, recv_sem, where):
    return pltpu.make_async_remote_copy(
        src_ref=src,
        dst_ref=dst,
        send_sem=send_sem,
        recv_sem=recv_sem,
        device_id=where,
        device_id_type=MESH,
    )


def pieces(refs_shape, count):
    planes, rows = refs_shape[0], refs_shape[1]
    per = max(1, count // planes)
    step = rows // per
    return [(p, pl.ds(h * step, step)) for p in range(planes) for h in range(per)]


def bin_kernel(
    nz, cuts, groups, tables, shots, in_ref, wt_ref, out_ref, held, terms, total, order, zs, zr
):
    z = lax.axis_index("rcv")
    stencil = wt_ref.shape[0] // 2
    rows = 2 * shots
    width = in_ref.shape[-1]
    cells = nz * groups

    def has(lane):
        near = z + 1 - 2 * lane
        return (near >= 0) & (near < nz)

    barrier = pltpu.get_barrier_semaphore()
    for lane in (0, 1):

        @pl.when(has(lane))
        def _():
            pl.semaphore_signal(
                barrier, inc=1, device_id={"rcv": z + 1 - 2 * lane}, device_id_type=MESH
            )

    pl.semaphore_wait(barrier, jnp.where(z > 0, 1, 0) + jnp.where(z < nz - 1, 1, 0))

    def along(own, block, lane, dist, q):
        cut = cuts[q]
        return remote(
            in_ref.at[cut] if own else held.at[(block,) + cut],
            held.at[(block,) + cut],
            zs.at[lane, dist, q],
            zr.at[lane, dist, q],
            {"rcv": z + 1 - 2 * lane},
        )

    for q in range(len(cuts)):
        for lane in (0, 1):

            @pl.when(has(lane))
            def _():
                along(True, z, lane, 0, q).start()

    w = wt_ref[...]
    w0 = w.astype(BF16)
    rest = w - w0.astype(F32)
    w1 = rest.astype(BF16)
    w2 = (rest - w1.astype(F32)).astype(BF16)
    table_ids = lax.broadcasted_iota(jnp.int32, (tables, width), 0).astype(F32)
    cell_ids = lax.broadcasted_iota(jnp.int32, (cells, width), 0).astype(F32)

    def sums(view):
        cell = view[0, rows : rows + 1, :] * float(groups) + view[0, rows + 1 : rows + 2, :]
        table_hot = (table_ids == view[0, rows + 2 : rows + 3, :]).astype(BF16)
        picked = sum(
            jnp.dot(part, table_hot, preferred_element_type=F32) for part in (w0, w1, w2)
        )
        hot = (cell_ids == cell).astype(BF16)
        real = view[0, 0:shots, :]
        imag = view[0, shots:rows, :]
        for j in range(stencil):
            wr = picked[j : j + 1, :]
            wi = picked[stencil + j : stencil + j + 1, :]
            base = j * 2 * rows
            for part, both in enumerate((real * wr - imag * wi, real * wi + imag * wr)):
                high, low = split(both)
                at = base + part * shots
                terms[at : at + shots, :] = high
                terms[at + rows : at + rows + shots, :] = low
        found = lax.dot_general(terms[...], hot, NT, preferred_element_type=F32)
        found = found.reshape(stencil, 2, rows, cells)
        return found[:, 0] + found[:, 1]

    total[...] = sums(in_ref)

    def hop(dist, carry):
        for q in range(len(cuts)):
            for lane in (0, 1):
                block = z - dist * (1 - 2 * lane)

                @pl.when((block >= 0) & (block < nz))
                def _():
                    along(False, block, lane, dist - 1, q).wait_recv()

                    @pl.when(has(lane))
                    def _():
                        along(False, block, lane, dist, q).start()

        def add(lane, inner):
            block = z - dist * (1 - 2 * lane)

            @pl.when((block >= 0) & (block < nz))
            def _():
                total[...] += sums(held.at[block])

            return inner

        return lax.fori_loop(0, 2, add, carry)

    lax.fori_loop(1, nz, hop, 0)
    for j in range(stencil):
        order[:, j, :] = total[j].T
    out_ref[...] = order[...].reshape(cells * stencil, rows).T

    def drain(dist, carry):
        for q in range(len(cuts)):
            for lane in (0, 1):
                block = z - dist * (1 - 2 * lane)

                @pl.when((block >= 0) & (block < nz) & has(lane))
                def _():
                    along(False, block, lane, dist, q).wait_send()

        return carry

    lax.fori_loop(0, nz, drain, 0)


def bin_all(value, moveout, nz, groups, shots, cid):
    tables, stencil = moveout.shape[1:]
    width = value.shape[-1]
    weights = jnp.transpose(moveout, (0, 2, 1)).reshape(2 * stencil, tables)
    cuts = pieces(value.shape, 3)
    dma = pltpu.SemaphoreType.DMA
    vmem = pl.BlockSpec(memory_space=pltpu.VMEM)
    out = pl.pallas_call(
        functools.partial(bin_kernel, nz, cuts, groups, tables, shots),
        out_shape=jax.ShapeDtypeStruct((2 * shots, nz * groups * stencil), F32),
        in_specs=[vmem, vmem],
        out_specs=vmem,
        scratch_shapes=[
            pltpu.VMEM((nz,) + value.shape, F32),
            pltpu.VMEM((stencil * 4 * shots, width), BF16),
            pltpu.VMEM((stencil, 2 * shots, nz * groups), F32),
            pltpu.VMEM((nz * groups, stencil, 2 * shots), F32),
            dma((2, nz, len(cuts))),
            dma((2, nz, len(cuts))),
        ],
        name="bin_all",
        compiler_params=pltpu.CompilerParams(
            collective_id=cid, has_side_effects=True, vmem_limit_bytes=56 << 20
        ),
    )(value, weights)
    return out.reshape(2, shots, nz * groups * stencil)


def spread_kernel(ns, in_ref, out_ref, ss, rs, ls):
    c = lax.axis_index("src")
    rows = in_ref.shape[1]
    width = out_ref.shape[2]
    barrier = pltpu.get_barrier_semaphore()
    for off in range(1, ns):
        pl.semaphore_signal(
            barrier, inc=1, device_id={"src": lax.rem(c + off, ns)}, device_id_type=MESH
        )
    pl.semaphore_wait(barrier, ns - 1)

    def part(who, p):
        return in_ref.at[p, :, pl.ds(pl.multiple_of(who * width, 128), width)]

    def place(who, p):
        return out_ref.at[p, pl.ds(pl.multiple_of(who * rows, 8), rows), :]

    sends = []
    for off in range(1, ns):
        for p in (0, 1):
            who = lax.rem(c + off, ns)
            copy = remote(
                part(who, p), place(c, p), ss.at[off - 1, p], rs.at[off - 1, p], {"src": who}
            )
            copy.start()
            sends.append(copy)
    own = [pltpu.make_async_copy(part(c, p), place(c, p), ls.at[p]) for p in (0, 1)]
    for copy in own:
        copy.start()
    for copy in own:
        copy.wait()
    for off in range(1, ns):
        for p in (0, 1):
            who = lax.rem(c + ns - off, ns)
            remote(
                place(who, p), place(who, p), ss.at[off - 1, p], rs.at[off - 1, p], {"src": who}
            ).wait_recv()
    for copy in sends:
        copy.wait_send()


def spread(value, ns, cid):
    _, rows, width = value.shape
    dma = pltpu.SemaphoreType.DMA
    vmem = pl.BlockSpec(memory_space=pltpu.VMEM)
    return pl.pallas_call(
        functools.partial(spread_kernel, ns),
        out_shape=jax.ShapeDtypeStruct((2, ns * rows, width // ns), F32),
        in_specs=[vmem],
        out_specs=vmem,
        scratch_shapes=[dma((ns - 1, 2)), dma((ns - 1, 2)), dma((2,))],
        name="spread",
        compiler_params=pltpu.CompilerParams(collective_id=cid, has_side_effects=True),
    )(value)


def sweeps_kernel(
    nz, ns, shots, tile, steps, fold,
    p_ref, b_ref, f_ref, a_ref, out_ref,
    a_all, high, low, mine, give, take, pass_on, got, own, held, cols, acc,
    a_sem, s1, r1, s2, r2, zs, zr, ps, pr, ls,
):
    z = lax.axis_index("rcv")
    c = lax.axis_index("src")
    core = lax.rem(c, 2)
    chip = c // 2
    chips = ns // 2
    half = ns * shots
    outs = steps * tile
    early = steps // 2
    last = steps + 1

    def a_copy(t):
        rows = pl.ds(pl.multiple_of(t * tile, tile), tile)
        return pltpu.make_async_copy(a_ref.at[:, rows, :], a_all.at[:, rows, :], a_sem.at[t])

    for t in range(min(2, steps)):
        a_copy(t).start()

    def has(lane):
        near = z + 1 - 2 * lane
        return (near >= 0) & (near < nz)

    barrier = pltpu.get_barrier_semaphore()
    for lane in (0, 1):

        @pl.when(has(lane))
        def _():
            pl.semaphore_signal(
                barrier, inc=1, device_id={"rcv": z + 1 - 2 * lane}, device_id_type=MESH
            )

    for off in range(1, ns):
        pl.semaphore_signal(
            barrier, inc=1, device_id={"src": lax.rem(c + off, ns)}, device_id_type=MESH
        )
    for part in (0, 1):
        top, rest = split(p_ref[part])
        high[part * half : (part + 1) * half, :] = top
        low[part * half : (part + 1) * half, :] = rest
    peers = jnp.where(z > 0, 1, 0) + jnp.where(z < nz - 1, 1, 0)
    pl.semaphore_wait(barrier, peers + ns - 1)

    def to_partner(sweep, t):
        return remote(
            give.at[sweep, t],
            take.at[sweep, t],
            s1.at[sweep, t],
            r1.at[sweep, t],
            {"src": c + 1 - 2 * core},
        )

    def to_chip(sweep, t, off):
        who = 2 * lax.rem(chip + off, chips) + core
        return remote(
            pass_on.at[sweep, t, off - 1],
            got.at[sweep, t, off - 1],
            s2.at[sweep, t, off - 1],
            r2.at[sweep, t, off - 1],
            {"src": who},
        )

    def times(t, ranges):
        rows = pl.ds(pl.multiple_of(t * tile, tile), tile)
        sums = []
        for part in (0, 1):
            total = None
            for cut in ranges:
                top, rest = split(a_all[part, rows, cut])
                now = lax.dot_general(high[:, cut], top, NT, preferred_element_type=F32)
                now += lax.dot_general(low[:, cut], top, NT, preferred_element_type=F32)
                now += lax.dot_general(high[:, cut], rest, NT, preferred_element_type=F32)
                total = now if total is None else total + now
            sums.append(total)
        return sums[0][:half] - sums[1][half:], sums[1][:half] + sums[0][half:]

    def hand_out(sweep, t, both):
        for part in (0, 1):
            for who in range(ns):
                value = both[part][who * shots : (who + 1) * shots]

                @pl.when(core == who % 2)
                def _():
                    mine[sweep, t, who // 2, part] = value

                @pl.when(core != who % 2)
                def _():
                    give[sweep, t, who // 2, part] = value

        to_partner(sweep, t).start()

    def reduce_pair(sweep, t):
        to_partner(sweep, t).wait_recv()
        for off in range(1, chips):
            there = lax.rem(chip + off, chips)
            pass_on[sweep, t, off - 1] = mine[sweep, t, there] + take[sweep, t, there]
            to_chip(sweep, t, off).start()
        mine[sweep, t, chip] += take[sweep, t, chip]

    def finish(sweep, t):
        found = mine[sweep, t, chip]
        for off in range(1, chips):
            to_chip(sweep, t, off).wait_recv()
            found += got[sweep, t, off - 1]
        at = pl.ds(pl.multiple_of(t * tile, tile), tile)
        fr, fi = f_ref[0, :, at], f_ref[1, :, at]
        return (
            b_ref[0, :, at] - (fr * found[0] - fi * found[1]),
            b_ref[1, :, at] - (fr * found[1] + fi * found[0]),
        )

    def along(src, block, lane, dist, t):
        return remote(
            src,
            held.at[block, t],
            zs.at[lane, dist, t],
            zr.at[lane, dist, t],
            {"rcv": z + 1 - 2 * lane},
        )

    def across(src, block, t):
        f = block - (block // fold) * fold
        return remote(
            src, cols.at[f, t, c], ps.at[block, t], pr.at[c, f, t], {"src": block // fold}
        )

    def local(src, block, t):
        f = block - (block // fold) * fold
        return pltpu.make_async_copy(src, cols.at[f, t, c], ls.at[f, t])

    def hand_on(src, block, t):
        @pl.when(block // fold != c)
        def _():
            across(src, block, t).start()

        @pl.when(block // fold == c)
        def _():
            local(src, block, t).start()

    def relay(t, dist):
        for lane in (0, 1):
            block = z - dist * (1 - 2 * lane)

            @pl.when((block >= 0) & (block < nz))
            def _():
                along(held.at[block, t], block, lane, dist - 1, t).wait_recv()

                @pl.when(has(lane))
                def _():
                    along(held.at[block, t], block, lane, dist, t).start()

                hand_on(held.at[block, t], block, t)

    def first(step, carry):
        @pl.when(step < steps)
        def _():
            a_copy(step).wait()

            @pl.when(step + 2 < steps)
            def _():
                a_copy(step + 2).start()

            hand_out(0, step, times(step, [pl.ds(0, fold * outs)]))

        @pl.when((step >= 1) & (step <= steps))
        def _():
            reduce_pair(0, step - 1)

        @pl.when(step >= 2)
        def _():
            t = step - 2
            real, imag = finish(0, t)
            own[t, 0] = real
            own[t, 1] = imag
            for lane in (0, 1):

                @pl.when(has(lane))
                def _():
                    along(own.at[t], z, lane, 0, t).start()

            hand_on(own.at[t], z, t)

        def earlier(dist, inner):
            t = step - 2 - 2 * dist

            @pl.when(t >= 0)
            def _():
                relay(t, dist)

            return inner

        return lax.fori_loop(1, nz, earlier, carry)

    lax.fori_loop(0, last + 1, first, 0)

    def rest_of(t):
        def each(dist, carry):
            @pl.when(t + 2 + 2 * dist > last)
            def _():
                relay(t, dist)

            return carry

        lax.fori_loop(1, nz, each, 0)

    def take_in(t, carry):
        for f in range(fold):
            local(own.at[t], c * fold + f, t).wait()
            for off in range(1, ns):
                who = lax.rem(c + off, ns)
                remote(
                    cols.at[f, t, who],
                    cols.at[f, t, who],
                    ps.at[0, t],
                    pr.at[who, f, t],
                    {"src": who},
                ).wait_recv()
            at = pl.ds(pl.multiple_of(f * outs + t * tile, tile), tile)
            for part in (0, 1):
                top, rest = split(cols[f, t, :, part].reshape(half, tile))
                high[part * half : (part + 1) * half, at] = top
                low[part * half : (part + 1) * half, at] = rest
        return carry

    def range_of(start, size):
        return [pl.ds(f * outs + start * tile, size * tile) for f in range(fold)]

    for t in range(early):
        rest_of(t)
    lax.fori_loop(0, early, take_in, 0)
    share = -(-steps // (steps - early))

    def between(t, carry):
        rest_of(t)

        def some(i, inner):
            r = (t - early) * share + i

            @pl.when(r < steps)
            def _():
                real, imag = times(r, range_of(0, early))
                acc[r, 0] = real
                acc[r, 1] = imag

            return inner

        return lax.fori_loop(0, share, some, carry)

    lax.fori_loop(early, steps, between, 0)
    lax.fori_loop(early, steps, take_in, 0)

    def second(step, carry):
        @pl.when(step < steps)
        def _():
            real, imag = times(step, range_of(early, steps - early))
            hand_out(1, step, (real + acc[step, 0], imag + acc[step, 1]))

        @pl.when((step >= 1) & (step <= steps))
        def _():
            reduce_pair(1, step - 1)

        @pl.when(step >= 2)
        def _():
            t = step - 2
            real, imag = finish(1, t)
            at = pl.ds(pl.multiple_of(t * tile, tile), tile)
            out_ref[0, :, at] = real
            out_ref[1, :, at] = imag

        return carry

    lax.fori_loop(0, last + 1, second, 0)

    def drain(t, carry):
        for sweep in (0, 1):
            to_partner(sweep, t).wait_send()
            for off in range(1, chips):
                to_chip(sweep, t, off).wait_send()

        def each(dist, inner):
            for lane in (0, 1):
                block = z - dist * (1 - 2 * lane)

                @pl.when((block >= 0) & (block < nz) & has(lane))
                def _():
                    along(held.at[block, t], block, lane, dist, t).wait_send()

            @pl.when(dist // fold != c)
            def _():
                across(held.at[dist, t], dist, t).wait_send()

            return inner

        return lax.fori_loop(0, nz, each, carry)

    lax.fori_loop(0, steps, drain, 0)


def two_sweeps(columns, binned, form, aperture, nz, ns, cid):
    _, half, depth = columns.shape
    outs = aperture.shape[1]
    shots = half // ns
    tile = min(outs, 256)
    steps = outs // tile
    chips = ns // 2
    fold = depth // outs
    dma = pltpu.SemaphoreType.DMA
    vmem = pl.BlockSpec(memory_space=pltpu.VMEM)
    block = (2, shots, tile)
    return pl.pallas_call(
        functools.partial(sweeps_kernel, nz, ns, shots, tile, steps, fold),
        out_shape=jax.ShapeDtypeStruct((2, shots, outs), F32),
        in_specs=[vmem, vmem, vmem, pl.BlockSpec(memory_space=pl.ANY)],
        out_specs=vmem,
        scratch_shapes=[
            pltpu.VMEM((2, outs, depth), F32),
            pltpu.VMEM((2 * half, depth), BF16),
            pltpu.VMEM((2 * half, depth), BF16),
            pltpu.VMEM((ITERS, steps, chips) + block, F32),
            pltpu.VMEM((ITERS, steps, chips) + block, F32),
            pltpu.VMEM((ITERS, steps, chips) + block, F32),
            pltpu.VMEM((ITERS, steps, chips - 1) + block, F32),
            pltpu.VMEM((ITERS, steps, chips - 1) + block, F32),
            pltpu.VMEM((steps,) + block, F32),
            pltpu.VMEM((nz, steps) + block, F32),
            pltpu.VMEM((fold, steps, ns) + block, F32),
            pltpu.VMEM((steps, 2, half, tile), F32),
            dma((steps,)),
            dma((ITERS, steps)),
            dma((ITERS, steps)),
            dma((ITERS, steps, chips - 1)),
            dma((ITERS, steps, chips - 1)),
            dma((2, nz, steps)),
            dma((2, nz, steps)),
            dma((nz, steps)),
            dma((ns, fold, steps)),
            dma((fold, steps)),
        ],
        name="two_sweeps",
        compiler_params=pltpu.CompilerParams(
            collective_id=cid, has_side_effects=True, vmem_limit_bytes=62 << 20
        ),
    )(columns, binned, form, aperture)


def per_device(nz, ns, traces, moveout, owner, group, table, aperture, shaping):
    groups = aperture.shape[1] // moveout.shape[2]
    shots = traces.shape[0]
    width = traces.shape[2]
    codes = jnp.stack([owner, group, table]).astype(F32)
    codes = jnp.concatenate([codes, jnp.zeros((5, width), F32)])
    flat = jnp.transpose(traces, (1, 0, 2)).reshape(2 * shots, width)
    everyone = bin_all(jnp.concatenate([flat, codes])[None], moveout, nz, groups, shots, 0)
    bins = aperture.shape[1]
    binned = lax.dynamic_slice_in_dim(everyone, lax.axis_index("rcv") * bins, bins, 2)
    form = jnp.transpose(shaping, (1, 0, 2))
    columns = spread(everyone, ns, 3)
    panel = two_sweeps(columns, binned, form, aperture, nz, ns, 2)
    return jnp.transpose(panel, (1, 0, 2))


def solution(mesh):
    nz, ns = mesh.shape["rcv"], mesh.shape["src"]
    in_specs = (
        P(("freq", "src"), None, "rcv"),
        P(None, "freq", None),
        P(("freq", "rcv")),
        P(("freq", "rcv")),
        P(("freq", "rcv")),
        P(None, ("freq", "rcv"), "src"),
        P(("freq", "src"), None, "rcv"),
    )
    out_specs = P(("freq", "src"), None, "rcv")
    return jax.shard_map(
        functools.partial(per_device, nz, ns),
        mesh=mesh,
        in_specs=in_specs,
        out_specs=out_specs,
        check_vma=False,
    )
```

```python
import functools

import jax
import jax.numpy as jnp
from jax import lax
from jax.experimental import pallas as pl
from jax.experimental.pallas import tpu as pltpu
from jax.sharding import PartitionSpec as P

ITERS = 2
SUB = 8
LANES = 128
SOON = 4
LAG = 3
HOP = 1
BEHIND = 4
MESH = pl.DeviceIdType.MESH
F32 = jnp.float32
BF16 = jnp.bfloat16
NT = (((1,), (1,)), ((), ()))


def split(value):
    high = value.astype(BF16)
    return high, (value - high.astype(F32)).astype(BF16)


def remote(src, dst, send_sem, recv_sem, where):
    return pltpu.make_async_remote_copy(
        src_ref=src,
        dst_ref=dst,
        send_sem=send_sem,
        recv_sem=recv_sem,
        device_id=where,
        device_id_type=MESH,
    )


def bin_kernel(
    nz, ns, groups, tables, fold,
    tr_ref, ow_ref, gr_ref, tb_ref, wt_ref, p_ref, b_ref,
    codes, held, hot, picked, terms, sums, got, order, order_own,
    cs, cr, zs, zr, ss, rs, ls,
):
    z = lax.axis_index("rcv")
    c = lax.axis_index("src")
    shots, _, width = tr_ref.shape
    stencil = wt_ref.shape[0] // 2
    chunks = shots // SUB
    cells = nz * groups
    share = cells // ns
    half = ns * shots

    def has(lane):
        near = z + 1 - 2 * lane
        return (near >= 0) & (near < nz)

    barrier = pltpu.get_barrier_semaphore()
    for lane in (0, 1):

        @pl.when(has(lane))
        def _():
            pl.semaphore_signal(
                barrier, inc=1, device_id={"rcv": z + 1 - 2 * lane}, device_id_type=MESH
            )

    for off in range(1, ns):
        pl.semaphore_signal(
            barrier, inc=1, device_id={"src": lax.rem(c + off, ns)}, device_id_type=MESH
        )
    codes[z, 0:1] = ow_ref[...]
    codes[z, 1:2] = gr_ref[...]
    codes[z, 2:3] = tb_ref[...]
    peers = jnp.where(z > 0, 1, 0) + jnp.where(z < nz - 1, 1, 0)
    pl.semaphore_wait(barrier, peers + ns - 1)

    def span(q):
        return pl.ds(pl.multiple_of(q * SUB, SUB), SUB)

    def along(own, block, lane, dist, q):
        return remote(
            tr_ref.at[span(q)] if own else held.at[block, span(q)],
            held.at[block, span(q)],
            zs.at[lane, dist, q],
            zr.at[lane, dist, q],
            {"rcv": z + 1 - 2 * lane},
        )

    def code(block, lane, dist):
        return remote(
            codes.at[block],
            codes.at[block],
            cs.at[lane, dist],
            cr.at[lane, dist],
            {"rcv": z + 1 - 2 * lane},
        )

    def columns(block):
        return pl.ds(pl.multiple_of(block * width, width), width)

    w = wt_ref[...]
    w0 = w.astype(BF16)
    rest = w - w0.astype(F32)
    w1 = rest.astype(BF16)
    w2 = (rest - w1.astype(F32)).astype(BF16)
    table_ids = lax.broadcasted_iota(jnp.int32, (tables, width), 0)
    cell_ids = lax.broadcasted_iota(jnp.int32, (cells, width), 0)

    def prepare(block):
        at = columns(block)
        cell = codes[block, 0:1] * groups + codes[block, 1:2]
        hot[:, at] = jnp.where(cell_ids == cell, 1.0, 0.0).astype(BF16)
        table_hot = jnp.where(table_ids == codes[block, 2:3], 1.0, 0.0).astype(BF16)
        picked[:, at] = sum(
            jnp.dot(part, table_hot, preferred_element_type=F32) for part in (w0, w1, w2)
        )

    def spread_terms(real, imag, block):
        at = columns(block)
        for j in range(stencil):
            wr = picked[j : j + 1, at]
            wi = picked[stencil + j : stencil + j + 1, at]
            both = jnp.concatenate([real * wr - imag * wi, real * wi + imag * wr])
            high, low = split(both)
            base = j * 4 * SUB
            terms[base : base + 2 * SUB, at] = high
            terms[base + 2 * SUB : base + 4 * SUB, at] = low

    def across(q, who):
        return remote(sums.at[q, who], got.at[q, c], ss.at[q, who], rs.at[q, c], {"src": who})

    def keep(q):
        return pltpu.make_async_copy(sums.at[q, c], got.at[q, c], ls.at[q])

    def chunk(q, carry):
        @pl.when(q == 0)
        def _():
            for lane in (0, 1):

                @pl.when(has(lane))
                def _():
                    code(z, lane, 0).start()
                    along(True, z, lane, 0, 0).start()

        @pl.when(q + 1 < chunks)
        def _():
            for lane in (0, 1):

                @pl.when(has(lane))
                def _():
                    along(True, z, lane, 0, q + 1).start()

        @pl.when(q == 0)
        def _():
            prepare(z)

        spread_terms(tr_ref[span(q), 0, :], tr_ref[span(q), 1, :], z)

        def hop(dist, inner):
            for lane in (0, 1):
                block = z - dist * (1 - 2 * lane)

                @pl.when((block >= 0) & (block < nz))
                def _():
                    @pl.when(q == 0)
                    def _():
                        code(block, lane, dist - 1).wait_recv()

                        @pl.when(has(lane))
                        def _():
                            code(block, lane, dist).start()

                    along(False, block, lane, dist - 1, q).wait_recv()

                    @pl.when(has(lane))
                    def _():
                        along(False, block, lane, dist, q).start()

            def add(lane, deeper):
                block = z - dist * (1 - 2 * lane)

                @pl.when((block >= 0) & (block < nz))
                def _():
                    @pl.when(q == 0)
                    def _():
                        prepare(block)

                    spread_terms(held[block, span(q), 0, :], held[block, span(q), 1, :], block)

                return deeper

            return lax.fori_loop(0, 2, add, inner)

        lax.fori_loop(1, nz, hop, 0)
        found = lax.dot_general(terms[...], hot[...], NT, preferred_element_type=F32)
        found = found.reshape(stencil, 2, 2 * SUB, cells)
        found = found[:, 0] + found[:, 1]
        for who in range(ns):
            sums[q, who] = found[:, :, who * share : (who + 1) * share]
        for off in range(ns - 1, 0, -1):
            across(q, lax.rem(c + off, ns)).start()
        keep(q).start()
        return carry

    lax.fori_loop(0, chunks, chunk, 0)

    who = z // fold
    for j in range(stencil):
        rows = jnp.concatenate(
            [sums[q, who, j, p * SUB : (p + 1) * SUB] for p in (0, 1) for q in range(chunks)]
        )
        lanes = jnp.concatenate([rows] * (LANES // (2 * shots))).T
        order_own[pl.ds(j, share, stride=stencil), :] = lanes
    outs = groups * stencil
    mine = order_own[pl.ds(pl.multiple_of((z - who * fold) * outs, outs), outs), :]
    b_ref[...] = mine.T[: 2 * shots].reshape(2, shots, outs)

    def settle(q, carry):
        keep(q).wait()
        for off in range(1, ns):
            peer = lax.rem(c + off, ns)
            remote(
                got.at[q, peer], got.at[q, peer], ss.at[q, peer], rs.at[q, peer], {"src": peer}
            ).wait_recv()
        return carry

    lax.fori_loop(0, chunks, settle, 0)
    for j in range(stencil):
        rows = jnp.concatenate(
            [
                got[q, peer, j, p * SUB : (p + 1) * SUB]
                for p in (0, 1)
                for peer in range(ns)
                for q in range(chunks)
            ]
        )
        for g in range(2 * half // LANES):
            order[g, pl.ds(j, share, stride=stencil), :] = rows[g * LANES : (g + 1) * LANES].T
    for g in range(2 * half // LANES):
        part, row = divmod(g * LANES, half)
        p_ref[part, row : row + LANES, :] = order[g].T

    def drain(q, carry):
        def each(dist, inner):
            for lane in (0, 1):
                block = z - dist * (1 - 2 * lane)

                @pl.when((block >= 0) & (block < nz) & has(lane))
                def _():
                    along(False, block, lane, dist, q).wait_send()

                    @pl.when(q == 0)
                    def _():
                        code(block, lane, dist).wait_send()

            return inner

        for off in range(1, ns):
            across(q, lax.rem(c + off, ns)).wait_send()
        return lax.fori_loop(0, nz, each, carry)

    lax.fori_loop(0, chunks, drain, 0)


def bin_all(traces, moveout, owner, group, table, nz, ns, bins, cid):
    tables, stencil = moveout.shape[1:]
    shots, _, width = traces.shape
    groups = bins // stencil
    fold = nz // ns
    chunks = shots // SUB
    share = nz * groups // ns
    weights = jnp.transpose(moveout, (0, 2, 1)).reshape(2 * stencil, tables)
    dma = pltpu.SemaphoreType.DMA
    vmem = pl.BlockSpec(memory_space=pltpu.VMEM)
    part = (chunks, ns, stencil, 2 * SUB, share)
    return pl.pallas_call(
        functools.partial(bin_kernel, nz, ns, groups, tables, fold),
        out_shape=(
            jax.ShapeDtypeStruct((2, ns * shots, share * stencil), F32),
            jax.ShapeDtypeStruct((2, shots, bins), F32),
        ),
        in_specs=[vmem] * 5,
        out_specs=(vmem, vmem),
        scratch_shapes=[
            pltpu.VMEM((nz, 3, width), jnp.int32),
            pltpu.VMEM((nz, shots, 2, width), F32),
            pltpu.VMEM((nz * groups, nz * width), BF16),
            pltpu.VMEM((2 * stencil, nz * width), F32),
            pltpu.VMEM((stencil * 4 * SUB, nz * width), BF16),
            pltpu.VMEM(part, F32),
            pltpu.VMEM(part, F32),
            pltpu.VMEM((2 * ns * shots // LANES, share * stencil, LANES), F32),
            pltpu.VMEM((share * stencil, LANES), F32),
            dma((2, nz)),
            dma((2, nz)),
            dma((2, nz, chunks)),
            dma((2, nz, chunks)),
            dma((chunks, ns)),
            dma((chunks, ns)),
            dma((chunks,)),
        ],
        name="bin_all",
        compiler_params=pltpu.CompilerParams(
            collective_id=cid, has_side_effects=True, vmem_limit_bytes=62 << 20
        ),
    )(traces, owner[None], group[None], table[None], weights)


def sweeps_kernel(
    nz, ns, shots, tile, steps, fold,
    p_ref, b_ref, f_ref, a_ref, out_ref,
    a_all, high, low, mine, give, take, pass_on, got, own, held, cols, acc,
    a_sem, s1, r1, s2, r2, zs, zr, ps, pr, ls,
):
    z = lax.axis_index("rcv")
    c = lax.axis_index("src")
    core = lax.rem(c, 2)
    chip = c // 2
    chips = ns // 2
    half = ns * shots
    outs = steps * tile
    early = steps // 2
    lag = LAG
    hop = HOP
    last = steps + lag - 1
    soon = SOON
    behind = BEHIND

    def a_copy(t):
        rows = pl.ds(pl.multiple_of(t * tile, tile), tile)
        return pltpu.make_async_copy(a_ref.at[:, rows, :], a_all.at[:, rows, :], a_sem.at[t])

    for t in range(min(2, steps)):
        a_copy(t).start()

    def has(lane):
        near = z + 1 - 2 * lane
        return (near >= 0) & (near < nz)

    barrier = pltpu.get_barrier_semaphore()
    for lane in (0, 1):

        @pl.when(has(lane))
        def _():
            pl.semaphore_signal(
                barrier, inc=1, device_id={"rcv": z + 1 - 2 * lane}, device_id_type=MESH
            )

    for off in range(1, ns):
        pl.semaphore_signal(
            barrier, inc=1, device_id={"src": lax.rem(c + off, ns)}, device_id_type=MESH
        )
    for part in (0, 1):
        top, rest = split(p_ref[part])
        high[part * half : (part + 1) * half, :] = top
        low[part * half : (part + 1) * half, :] = rest
    peers = jnp.where(z > 0, 1, 0) + jnp.where(z < nz - 1, 1, 0)
    pl.semaphore_wait(barrier, peers + ns - 1)

    def to_partner(sweep, t):
        return remote(
            give.at[sweep, t],
            take.at[sweep, t],
            s1.at[sweep, t],
            r1.at[sweep, t],
            {"src": c + 1 - 2 * core},
        )

    def to_chip(sweep, t, off):
        who = 2 * lax.rem(chip + off, chips) + core
        return remote(
            pass_on.at[sweep, t, off - 1],
            got.at[sweep, t, off - 1],
            s2.at[sweep, t, off - 1],
            r2.at[sweep, t, off - 1],
            {"src": who},
        )

    def times(t, ranges):
        rows = pl.ds(pl.multiple_of(t * tile, tile), tile)
        sums = []
        for part in (0, 1):
            total = None
            for cut in ranges:
                top, rest = split(a_all[part, rows, cut])
                now = lax.dot_general(high[:, cut], top, NT, preferred_element_type=F32)
                now += lax.dot_general(low[:, cut], top, NT, preferred_element_type=F32)
                now += lax.dot_general(high[:, cut], rest, NT, preferred_element_type=F32)
                total = now if total is None else total + now
            sums.append(total)
        return sums[0][:half] - sums[1][half:], sums[1][:half] + sums[0][half:]

    def hand_out(sweep, t, both):
        for part in (0, 1):
            for who in range(ns):
                value = both[part][who * shots : (who + 1) * shots]

                @pl.when(core == who % 2)
                def _():
                    mine[sweep, t, who // 2, part] = value

                @pl.when(core != who % 2)
                def _():
                    give[sweep, t, who // 2, part] = value

        to_partner(sweep, t).start()

    def reduce_pair(sweep, t):
        to_partner(sweep, t).wait_recv()
        for off in range(1, chips):
            there = lax.rem(chip + off, chips)
            pass_on[sweep, t, off - 1] = mine[sweep, t, there] + take[sweep, t, there]
            to_chip(sweep, t, off).start()
        mine[sweep, t, chip] += take[sweep, t, chip]

    def finish(sweep, t):
        found = mine[sweep, t, chip]
        for off in range(1, chips):
            to_chip(sweep, t, off).wait_recv()
            found += got[sweep, t, off - 1]
        at = pl.ds(pl.multiple_of(t * tile, tile), tile)
        fr, fi = f_ref[0, :, at], f_ref[1, :, at]
        return (
            b_ref[0, :, at] - (fr * found[0] - fi * found[1]),
            b_ref[1, :, at] - (fr * found[1] + fi * found[0]),
        )

    def along(src, block, lane, dist, t):
        return remote(
            src,
            held.at[block, t],
            zs.at[lane, dist, t],
            zr.at[lane, dist, t],
            {"rcv": z + 1 - 2 * lane},
        )

    def across(src, block, t):
        f = block - (block // fold) * fold
        return remote(
            src, cols.at[f, t, c], ps.at[block, t], pr.at[c, f, t], {"src": block // fold}
        )

    def local(src, block, t):
        f = block - (block // fold) * fold
        return pltpu.make_async_copy(src, cols.at[f, t, c], ls.at[f, t])

    def hand_on(src, block, t):
        @pl.when(block // fold != c)
        def _():
            across(src, block, t).start()

        @pl.when(block // fold == c)
        def _():
            local(src, block, t).start()

    def relay(t, dist, fresh, give_it):
        for lane in (0, 1):
            block = z - dist * (1 - 2 * lane)

            @pl.when((block >= 0) & (block < nz))
            def _():
                @pl.when(jnp.asarray(fresh))
                def _():
                    along(held.at[block, t], block, lane, dist - 1, t).wait_recv()

                    @pl.when(has(lane))
                    def _():
                        along(held.at[block, t], block, lane, dist, t).start()

                @pl.when(jnp.asarray(give_it))
                def _():
                    hand_on(held.at[block, t], block, t)

    def first(step, carry):
        @pl.when(step < steps)
        def _():
            a_copy(step).wait()

            @pl.when(step + 2 < steps)
            def _():
                a_copy(step + 2).start()

            hand_out(0, step, times(step, [pl.ds(0, fold * outs)]))

        @pl.when((step >= 1) & (step <= steps))
        def _():
            reduce_pair(0, step - 1)

        @pl.when(step >= lag)
        def _():
            t = step - lag
            real, imag = finish(0, t)
            own[t, 0] = real
            own[t, 1] = imag
            for lane in (0, 1):

                @pl.when(has(lane))
                def _():
                    along(own.at[t], z, lane, 0, t).start()

            @pl.when(t < soon)
            def _():
                hand_on(own.at[t], z, t)

        def earlier(dist, inner):
            t = step - lag - hop * dist

            @pl.when(t >= 0)
            def _():
                relay(t, dist, True, t < soon)

            return inner

        return lax.fori_loop(1, nz, earlier, carry)

    lax.fori_loop(0, last + 1, first, 0)

    def rest_of(t):
        @pl.when(t >= soon)
        def _():
            hand_on(own.at[t], z, t)

        def each(dist, carry):
            fresh = t + lag + hop * dist > last
            relay(t, dist, fresh, fresh | (t >= soon))
            return carry

        lax.fori_loop(1, nz, each, 0)

    def take_in(t, carry):
        for f in range(fold):
            local(own.at[t], c * fold + f, t).wait()
            for off in range(1, ns):
                who = lax.rem(c + off, ns)
                remote(
                    cols.at[f, t, who],
                    cols.at[f, t, who],
                    ps.at[0, t],
                    pr.at[who, f, t],
                    {"src": who},
                ).wait_recv()
            at = pl.ds(pl.multiple_of(f * outs + t * tile, tile), tile)
            for part in (0, 1):
                top, rest = split(cols[f, t, :, part].reshape(half, tile))
                high[part * half : (part + 1) * half, at] = top
                low[part * half : (part + 1) * half, at] = rest
        return carry

    def range_of(start, size):
        return [pl.ds(f * outs + start * tile, size * tile) for f in range(fold)]

    for t in range(early):
        rest_of(t)
    lax.fori_loop(0, early, take_in, 0)
    share = -(-steps // (steps - early))

    def between(t, carry):
        rest_of(t)

        def some(i, inner):
            r = (t - early) * share + i

            @pl.when(r < steps)
            def _():
                real, imag = times(r, range_of(0, early))
                acc[r, 0] = real
                acc[r, 1] = imag

            return inner

        return lax.fori_loop(0, share, some, carry)

    lax.fori_loop(early, steps, between, 0)
    lax.fori_loop(early, steps, take_in, 0)

    def second(step, carry):
        @pl.when(step < steps)
        def _():
            real, imag = times(step, range_of(early, steps - early))
            hand_out(1, step, (real + acc[step, 0], imag + acc[step, 1]))

        @pl.when((step >= 1) & (step <= steps))
        def _():
            reduce_pair(1, step - 1)

        @pl.when(step >= behind)
        def _():
            t = step - behind
            real, imag = finish(1, t)
            at = pl.ds(pl.multiple_of(t * tile, tile), tile)
            out_ref[0, :, at] = real
            out_ref[1, :, at] = imag

        return carry

    lax.fori_loop(0, steps + behind, second, 0)

    def drain(t, carry):
        for sweep in (0, 1):
            to_partner(sweep, t).wait_send()
            for off in range(1, chips):
                to_chip(sweep, t, off).wait_send()

        def each(dist, inner):
            for lane in (0, 1):
                block = z - dist * (1 - 2 * lane)

                @pl.when((block >= 0) & (block < nz) & has(lane))
                def _():
                    along(held.at[block, t], block, lane, dist, t).wait_send()

            @pl.when(dist // fold != c)
            def _():
                across(held.at[dist, t], dist, t).wait_send()

            return inner

        return lax.fori_loop(0, nz, each, carry)

    lax.fori_loop(0, steps, drain, 0)


def two_sweeps(columns, binned, form, aperture, nz, ns, cid):
    _, half, depth = columns.shape
    outs = aperture.shape[1]
    shots = half // ns
    tile = min(outs, 256)
    steps = outs // tile
    chips = ns // 2
    fold = depth // outs
    dma = pltpu.SemaphoreType.DMA
    vmem = pl.BlockSpec(memory_space=pltpu.VMEM)
    block = (2, shots, tile)
    return pl.pallas_call(
        functools.partial(sweeps_kernel, nz, ns, shots, tile, steps, fold),
        out_shape=jax.ShapeDtypeStruct((2, shots, outs), F32),
        in_specs=[vmem, vmem, vmem, pl.BlockSpec(memory_space=pl.ANY)],
        out_specs=vmem,
        scratch_shapes=[
            pltpu.VMEM((2, outs, depth), F32),
            pltpu.VMEM((2 * half, depth), BF16),
            pltpu.VMEM((2 * half, depth), BF16),
            pltpu.VMEM((ITERS, steps, chips) + block, F32),
            pltpu.VMEM((ITERS, steps, chips) + block, F32),
            pltpu.VMEM((ITERS, steps, chips) + block, F32),
            pltpu.VMEM((ITERS, steps, chips - 1) + block, F32),
            pltpu.VMEM((ITERS, steps, chips - 1) + block, F32),
            pltpu.VMEM((steps,) + block, F32),
            pltpu.VMEM((nz, steps) + block, F32),
            pltpu.VMEM((fold, steps, ns) + block, F32),
            pltpu.VMEM((steps, 2, half, tile), F32),
            dma((steps,)),
            dma((ITERS, steps)),
            dma((ITERS, steps)),
            dma((ITERS, steps, chips - 1)),
            dma((ITERS, steps, chips - 1)),
            dma((2, nz, steps)),
            dma((2, nz, steps)),
            dma((nz, steps)),
            dma((ns, fold, steps)),
            dma((fold, steps)),
        ],
        name="two_sweeps",
        compiler_params=pltpu.CompilerParams(
            collective_id=cid, has_side_effects=True, vmem_limit_bytes=62 << 20
        ),
    )(columns, binned, form, aperture)


def per_device(nz, ns, traces, moveout, owner, group, table, aperture, shaping):
    bins = aperture.shape[1]
    columns, binned = bin_all(traces, moveout, owner, group, table, nz, ns, bins, 0)
    form = jnp.transpose(shaping, (1, 0, 2))
    panel = two_sweeps(columns, binned, form, aperture, nz, ns, 2)
    return jnp.transpose(panel, (1, 0, 2))


def solution(mesh):
    nz, ns = mesh.shape["rcv"], mesh.shape["src"]
    in_specs = (
        P(("freq", "src"), None, "rcv"),
        P(None, "freq", None),
        P(("freq", "rcv")),
        P(("freq", "rcv")),
        P(("freq", "rcv")),
        P(None, ("freq", "rcv"), "src"),
        P(("freq", "src"), None, "rcv"),
    )
    out_specs = P(("freq", "src"), None, "rcv")
    return jax.shard_map(
        functools.partial(per_device, nz, ns),
        mesh=mesh,
        in_specs=in_specs,
        out_specs=out_specs,
        check_vma=False,
    )
```

```python
import functools

import jax
import jax.numpy as jnp
from jax import lax
from jax.experimental import pallas as pl
from jax.experimental.pallas import tpu as pltpu
from jax.sharding import PartitionSpec as P

ITERS = 2
SUB = 8
LANES = 128
SOON = 4
LAG = 3
HOP = 1
BEHIND = 4
MESH = pl.DeviceIdType.MESH
F32 = jnp.float32
BF16 = jnp.bfloat16
NT = (((1,), (1,)), ((), ()))


def split(value):
    high = value.astype(BF16)
    return high, (value - high.astype(F32)).astype(BF16)


def remote(src, dst, send_sem, recv_sem, where):
    return pltpu.make_async_remote_copy(
        src_ref=src,
        dst_ref=dst,
        send_sem=send_sem,
        recv_sem=recv_sem,
        device_id=where,
        device_id_type=MESH,
    )


def kernel(
    nz, ns, groups, tables, fold, tile, steps,
    tr_ref, ow_ref, gr_ref, tb_ref, wt_ref, f_ref, a_ref, out_ref,
    codes, near, hot, picked, terms, found, sums, bins, order, b_own,
    a_all, high, low, mine, give, take, pass_on, got, own, held, cols, acc,
    cs, cr, ts, tr, xs, xr, xl,
    a_sem, s1, r1, s2, r2, zs, zr, ps, pr, ls,
):
    z = lax.axis_index("rcv")
    c = lax.axis_index("src")
    core = lax.rem(c, 2)
    chip = c // 2
    chips = ns // 2
    shots, _, width = tr_ref.shape
    stencil = wt_ref.shape[0] // 2
    chunks = shots // SUB
    cells = nz * groups
    share = cells // ns
    half = ns * shots
    outs = steps * tile
    early = steps // 2
    lag = LAG
    hop = HOP
    soon = SOON
    behind = BEHIND
    last = steps + lag - 1

    def a_copy(t):
        rows = pl.ds(pl.multiple_of(t * tile, tile), tile)
        return pltpu.make_async_copy(a_ref.at[:, rows, :], a_all.at[:, rows, :], a_sem.at[t])

    for t in range(min(2, steps)):
        a_copy(t).start()

    def has(lane):
        other = z + 1 - 2 * lane
        return (other >= 0) & (other < nz)

    barrier = pltpu.get_barrier_semaphore()
    for lane in (0, 1):

        @pl.when(has(lane))
        def _():
            pl.semaphore_signal(
                barrier, inc=1, device_id={"rcv": z + 1 - 2 * lane}, device_id_type=MESH
            )

    for off in range(1, ns):
        pl.semaphore_signal(
            barrier, inc=1, device_id={"src": lax.rem(c + off, ns)}, device_id_type=MESH
        )
    codes[z, 0:1] = ow_ref[...]
    codes[z, 1:2] = gr_ref[...]
    codes[z, 2:3] = tb_ref[...]
    peers = jnp.where(z > 0, 1, 0) + jnp.where(z < nz - 1, 1, 0)
    pl.semaphore_wait(barrier, peers + ns - 1)

    def span(q):
        return pl.ds(pl.multiple_of(q * SUB, SUB), SUB)

    def raw(own, block, lane, dist, q):
        return remote(
            tr_ref.at[span(q)] if own else near.at[block, span(q)],
            near.at[block, span(q)],
            ts.at[lane, dist, q],
            tr.at[lane, dist, q],
            {"rcv": z + 1 - 2 * lane},
        )

    def code(block, lane, dist):
        return remote(
            codes.at[block],
            codes.at[block],
            cs.at[lane, dist],
            cr.at[lane, dist],
            {"rcv": z + 1 - 2 * lane},
        )

    w = wt_ref[...]
    w0 = w.astype(BF16)
    rest = w - w0.astype(F32)
    w1 = rest.astype(BF16)
    w2 = (rest - w1.astype(F32)).astype(BF16)
    table_ids = lax.broadcasted_iota(jnp.int32, (tables, width), 0)
    cell_ids = lax.broadcasted_iota(jnp.int32, (cells, width), 0)

    def prepare(block):
        cell = codes[block, 0:1] * groups + codes[block, 1:2]
        hot[block] = jnp.where(cell_ids == cell, 1.0, 0.0).astype(BF16)
        table_hot = jnp.where(table_ids == codes[block, 2:3], 1.0, 0.0).astype(BF16)
        picked[block] = sum(
            jnp.dot(part, table_hot, preferred_element_type=F32) for part in (w0, w1, w2)
        )

    def add_in(real, imag, block, start):
        for j in range(stencil):
            wr = picked[block, j : j + 1]
            wi = picked[block, stencil + j : stencil + j + 1]
            both = jnp.concatenate([real * wr - imag * wi, real * wi + imag * wr])
            top, rest = split(both)
            base = j * 4 * SUB
            terms[base : base + 2 * SUB, :] = top
            terms[base + 2 * SUB : base + 4 * SUB, :] = rest
        now = lax.dot_general(terms[...], hot[block], NT, preferred_element_type=F32)
        found[...] = now if start else found[...] + now

    def swap(q, who):
        return remote(sums.at[q, who], bins.at[q, c], xs.at[q, who], xr.at[q, c], {"src": who})

    def keep(q):
        return pltpu.make_async_copy(sums.at[q, c], bins.at[q, c], xl.at[q])

    def relay_in(q, dist):
        for lane in (0, 1):
            block = z - dist * (1 - 2 * lane)

            @pl.when((block >= 0) & (block < nz))
            def _():
                @pl.when(jnp.asarray(q == 0))
                def _():
                    code(block, lane, dist - 1).wait_recv()

                    @pl.when(has(lane))
                    def _():
                        code(block, lane, dist).start()

                raw(False, block, lane, dist - 1, q).wait_recv()

                @pl.when(has(lane))
                def _():
                    raw(False, block, lane, dist, q).start()

    def chunk(q, carry):
        @pl.when(q == 0)
        def _():
            for lane in (0, 1):

                @pl.when(has(lane))
                def _():
                    code(z, lane, 0).start()
                    raw(True, z, lane, 0, 0).start()

        @pl.when(q + 1 < chunks)
        def _():
            for lane in (0, 1):

                @pl.when(has(lane))
                def _():
                    raw(True, z, lane, 0, q + 1).start()

        @pl.when(q == 0)
        def _():
            prepare(z)

        add_in(tr_ref[span(q), 0, :], tr_ref[span(q), 1, :], z, True)

        def hop_in(dist, inner):
            @pl.when((q == 0) | (dist > 1))
            def _():
                relay_in(q, dist)

            @pl.when((dist == nz - 1) & (q + 1 < chunks))
            def _():
                relay_in(q + 1, 1)

            def add(lane, deeper):
                block = z - dist * (1 - 2 * lane)

                @pl.when((block >= 0) & (block < nz))
                def _():
                    @pl.when(q == 0)
                    def _():
                        prepare(block)

                    add_in(near[block, span(q), 0, :], near[block, span(q), 1, :], block, False)

                return deeper

            return lax.fori_loop(0, 2, add, inner)

        lax.fori_loop(1, nz, hop_in, 0)
        both = found[...].reshape(stencil, 2, 2 * SUB, cells)
        both = both[:, 0] + both[:, 1]
        for who in range(ns):
            sums[q, who] = both[:, :, who * share : (who + 1) * share]
        for off in range(ns - 1, 0, -1):
            swap(q, lax.rem(c + off, ns)).start()
        keep(q).start()
        return carry

    lax.fori_loop(0, chunks, chunk, 0)

    who = z // fold
    for j in range(stencil):
        rows = jnp.concatenate(
            [sums[q, who, j, p * SUB : (p + 1) * SUB] for p in (0, 1) for q in range(chunks)]
        )
        lanes = jnp.concatenate([rows] * (LANES // (2 * shots))).T
        order[0, pl.ds(j, share, stride=stencil), :] = lanes
    base = order[0, pl.ds(pl.multiple_of((z - who * fold) * outs, outs), outs), :]
    b_own[...] = base.T[: 2 * shots].reshape(2, shots, outs)

    def settle(q, carry):
        keep(q).wait()
        for off in range(1, ns):
            peer = lax.rem(c + off, ns)
            remote(
                bins.at[q, peer], bins.at[q, peer], xs.at[q, peer], xr.at[q, peer], {"src": peer}
            ).wait_recv()
        return carry

    lax.fori_loop(0, chunks, settle, 0)
    for j in range(stencil):
        rows = jnp.concatenate(
            [
                bins[q, peer, j, p * SUB : (p + 1) * SUB]
                for p in (0, 1)
                for peer in range(ns)
                for q in range(chunks)
            ]
        )
        for g in range(2 * half // LANES):
            order[g, pl.ds(j, share, stride=stencil), :] = rows[g * LANES : (g + 1) * LANES].T
    for g in range(2 * half // LANES):
        part, row = divmod(g * LANES, half)
        top, rest = split(order[g].T)
        high[part * half + row : part * half + row + LANES, :] = top
        low[part * half + row : part * half + row + LANES, :] = rest

    def to_partner(sweep, t):
        return remote(
            give.at[t],
            take.at[t],
            s1.at[sweep, t],
            r1.at[sweep, t],
            {"src": c + 1 - 2 * core},
        )

    def to_chip(sweep, t, off):
        who = 2 * lax.rem(chip + off, chips) + core
        return remote(
            pass_on.at[t, off - 1],
            got.at[t, off - 1],
            s2.at[sweep, t, off - 1],
            r2.at[sweep, t, off - 1],
            {"src": who},
        )

    def times(t, ranges):
        rows = pl.ds(pl.multiple_of(t * tile, tile), tile)
        sums = []
        for part in (0, 1):
            total = None
            for cut in ranges:
                top, rest = split(a_all[part, rows, cut])
                now = lax.dot_general(high[:, cut], top, NT, preferred_element_type=F32)
                now += lax.dot_general(low[:, cut], top, NT, preferred_element_type=F32)
                now += lax.dot_general(high[:, cut], rest, NT, preferred_element_type=F32)
                total = now if total is None else total + now
            sums.append(total)
        return sums[0][:half] - sums[1][half:], sums[1][:half] + sums[0][half:]

    def hand_out(sweep, t, both):
        for part in (0, 1):
            for who in range(ns):
                value = both[part][who * shots : (who + 1) * shots]

                @pl.when(core == who % 2)
                def _():
                    mine[t, who // 2, part] = value

                @pl.when(core != who % 2)
                def _():
                    give[t, who // 2, part] = value

        to_partner(sweep, t).start()

    def reduce_pair(sweep, t):
        to_partner(sweep, t).wait_recv()
        for off in range(1, chips):
            there = lax.rem(chip + off, chips)
            pass_on[t, off - 1] = mine[t, there] + take[t, there]
            to_chip(sweep, t, off).start()
        mine[t, chip] += take[t, chip]

    def finish(sweep, t):
        found = mine[t, chip]
        for off in range(1, chips):
            to_chip(sweep, t, off).wait_recv()
            found += got[t, off - 1]
        at = pl.ds(pl.multiple_of(t * tile, tile), tile)
        fr, fi = f_ref[:, 0, at], f_ref[:, 1, at]
        return (
            b_own[0, :, at] - (fr * found[0] - fi * found[1]),
            b_own[1, :, at] - (fr * found[1] + fi * found[0]),
        )

    def along(src, block, lane, dist, t):
        return remote(
            src,
            held.at[block, t],
            zs.at[lane, dist, t],
            zr.at[lane, dist, t],
            {"rcv": z + 1 - 2 * lane},
        )

    def across(src, block, t):
        f = block - (block // fold) * fold
        return remote(
            src, cols.at[f, t, c], ps.at[block, t], pr.at[c, f, t], {"src": block // fold}
        )

    def local(src, block, t):
        f = block - (block // fold) * fold
        return pltpu.make_async_copy(src, cols.at[f, t, c], ls.at[f, t])

    def hand_on(src, block, t):
        @pl.when(block // fold != c)
        def _():
            across(src, block, t).start()

        @pl.when(block // fold == c)
        def _():
            local(src, block, t).start()

    def relay(t, dist, fresh, give_it):
        for lane in (0, 1):
            block = z - dist * (1 - 2 * lane)

            @pl.when((block >= 0) & (block < nz))
            def _():
                @pl.when(jnp.asarray(fresh))
                def _():
                    along(held.at[block, t], block, lane, dist - 1, t).wait_recv()

                    @pl.when(has(lane))
                    def _():
                        along(held.at[block, t], block, lane, dist, t).start()

                @pl.when(jnp.asarray(give_it))
                def _():
                    hand_on(held.at[block, t], block, t)

    def first(step, carry):
        @pl.when(step < steps)
        def _():
            a_copy(step).wait()

            @pl.when(step + 2 < steps)
            def _():
                a_copy(step + 2).start()

            hand_out(0, step, times(step, [pl.ds(0, fold * outs)]))

        @pl.when((step >= 1) & (step <= steps))
        def _():
            reduce_pair(0, step - 1)

        @pl.when(step >= lag)
        def _():
            t = step - lag
            real, imag = finish(0, t)
            own[t, 0] = real
            own[t, 1] = imag
            for lane in (0, 1):

                @pl.when(has(lane))
                def _():
                    along(own.at[t], z, lane, 0, t).start()

            @pl.when(t < soon)
            def _():
                hand_on(own.at[t], z, t)

        def earlier(dist, inner):
            t = step - lag - hop * dist

            @pl.when(t >= 0)
            def _():
                relay(t, dist, True, t < soon)

            return inner

        return lax.fori_loop(1, nz, earlier, carry)

    lax.fori_loop(0, last + 1, first, 0)

    def rest_of(t):
        @pl.when(t >= soon)
        def _():
            hand_on(own.at[t], z, t)

        def each(dist, carry):
            fresh = t + lag + hop * dist > last
            relay(t, dist, fresh, fresh | (t >= soon))
            return carry

        lax.fori_loop(1, nz, each, 0)

    def take_in(t, carry):
        for f in range(fold):
            local(own.at[t], c * fold + f, t).wait()
            for off in range(1, ns):
                who = lax.rem(c + off, ns)
                remote(
                    cols.at[f, t, who],
                    cols.at[f, t, who],
                    ps.at[0, t],
                    pr.at[who, f, t],
                    {"src": who},
                ).wait_recv()
            at = pl.ds(pl.multiple_of(f * outs + t * tile, tile), tile)
            for part in (0, 1):
                top, rest = split(cols[f, t, :, part].reshape(half, tile))
                high[part * half : (part + 1) * half, at] = top
                low[part * half : (part + 1) * half, at] = rest
        return carry

    def range_of(start, size):
        return [pl.ds(f * outs + start * tile, size * tile) for f in range(fold)]

    for t in range(early):
        rest_of(t)
    lax.fori_loop(0, early, take_in, 0)
    share = -(-steps // (steps - early))

    def between(t, carry):
        rest_of(t)

        def some(i, inner):
            r = (t - early) * share + i

            @pl.when(r < steps)
            def _():
                real, imag = times(r, range_of(0, early))
                acc[r, 0] = real
                acc[r, 1] = imag

            return inner

        return lax.fori_loop(0, share, some, carry)

    lax.fori_loop(early, steps, between, 0)
    lax.fori_loop(early, steps, take_in, 0)

    def sent(t, carry):
        to_partner(0, t).wait_send()
        for off in range(1, chips):
            to_chip(0, t, off).wait_send()
        return carry

    lax.fori_loop(0, steps, sent, 0)

    def second(step, carry):
        @pl.when(step < steps)
        def _():
            real, imag = times(step, range_of(early, steps - early))
            hand_out(1, step, (real + acc[step, 0], imag + acc[step, 1]))

        @pl.when((step >= 1) & (step <= steps))
        def _():
            reduce_pair(1, step - 1)

        @pl.when(step >= behind)
        def _():
            t = step - behind
            real, imag = finish(1, t)
            at = pl.ds(pl.multiple_of(t * tile, tile), tile)
            out_ref[:, 0, at] = real
            out_ref[:, 1, at] = imag

        return carry

    lax.fori_loop(0, steps + behind, second, 0)

    def drain(t, carry):
        to_partner(1, t).wait_send()
        for off in range(1, chips):
            to_chip(1, t, off).wait_send()

        def each(dist, inner):
            for lane in (0, 1):
                block = z - dist * (1 - 2 * lane)

                @pl.when((block >= 0) & (block < nz) & has(lane))
                def _():
                    along(held.at[block, t], block, lane, dist, t).wait_send()

            @pl.when(dist // fold != c)
            def _():
                across(held.at[dist, t], dist, t).wait_send()

            return inner

        return lax.fori_loop(0, nz, each, carry)

    lax.fori_loop(0, steps, drain, 0)

    def drain_in(q, carry):
        def each(dist, inner):
            for lane in (0, 1):
                block = z - dist * (1 - 2 * lane)

                @pl.when((block >= 0) & (block < nz) & has(lane))
                def _():
                    raw(False, block, lane, dist, q).wait_send()

                    @pl.when(q == 0)
                    def _():
                        code(block, lane, dist).wait_send()

            return inner

        for off in range(1, ns):
            swap(q, lax.rem(c + off, ns)).wait_send()
        return lax.fori_loop(0, nz, each, carry)

    lax.fori_loop(0, chunks, drain_in, 0)


def predict(traces, moveout, owner, group, table, aperture, shaping, nz, ns):
    tables, stencil = moveout.shape[1:]
    shots, _, width = traces.shape
    _, outs, depth = aperture.shape
    groups = outs // stencil
    fold = nz // ns
    chunks = shots // SUB
    cells = nz * groups
    share = cells // ns
    half = ns * shots
    tile = min(outs, 256)
    steps = outs // tile
    chips = ns // 2
    weights = jnp.transpose(moveout, (0, 2, 1)).reshape(2 * stencil, tables)
    dma = pltpu.SemaphoreType.DMA
    vmem = pl.BlockSpec(memory_space=pltpu.VMEM)
    part = (chunks, ns, stencil, 2 * SUB, share)
    block = (2, shots, tile)
    return pl.pallas_call(
        functools.partial(kernel, nz, ns, groups, tables, fold, tile, steps),
        out_shape=jax.ShapeDtypeStruct((shots, 2, outs), F32),
        in_specs=[vmem] * 6 + [pl.BlockSpec(memory_space=pl.ANY)],
        out_specs=vmem,
        scratch_shapes=[
            pltpu.VMEM((nz, 3, width), jnp.int32),
            pltpu.VMEM((nz, shots, 2, width), F32),
            pltpu.VMEM((nz, cells, width), BF16),
            pltpu.VMEM((nz, 2 * stencil, width), F32),
            pltpu.VMEM((stencil * 4 * SUB, width), BF16),
            pltpu.VMEM((stencil * 4 * SUB, cells), F32),
            pltpu.VMEM(part, F32),
            pltpu.VMEM(part, F32),
            pltpu.VMEM((2 * half // LANES, share * stencil, LANES), F32),
            pltpu.VMEM((2, shots, outs), F32),
            pltpu.VMEM((2, outs, depth), F32),
            pltpu.VMEM((2 * half, depth), BF16),
            pltpu.VMEM((2 * half, depth), BF16),
            pltpu.VMEM((steps, chips) + block, F32),
            pltpu.VMEM((steps, chips) + block, F32),
            pltpu.VMEM((steps, chips) + block, F32),
            pltpu.VMEM((steps, chips - 1) + block, F32),
            pltpu.VMEM((steps, chips - 1) + block, F32),
            pltpu.VMEM((steps,) + block, F32),
            pltpu.VMEM((nz, steps) + block, F32),
            pltpu.VMEM((fold, steps, ns) + block, F32),
            pltpu.VMEM((steps, 2, half, tile), F32),
            dma((2, nz)),
            dma((2, nz)),
            dma((2, nz, chunks)),
            dma((2, nz, chunks)),
            dma((chunks, ns)),
            dma((chunks, ns)),
            dma((chunks,)),
            dma((steps,)),
            dma((ITERS, steps)),
            dma((ITERS, steps)),
            dma((ITERS, steps, chips - 1)),
            dma((ITERS, steps, chips - 1)),
            dma((2, nz, steps)),
            dma((2, nz, steps)),
            dma((nz, steps)),
            dma((ns, fold, steps)),
            dma((fold, steps)),
        ],
        name="predict",
        compiler_params=pltpu.CompilerParams(
            collective_id=0, has_side_effects=True, vmem_limit_bytes=67043328
        ),
    )(traces, owner[None], group[None], table[None], weights, shaping, aperture)


def per_device(nz, ns, traces, moveout, owner, group, table, aperture, shaping):
    return predict(traces, moveout, owner, group, table, aperture, shaping, nz, ns)


def solution(mesh):
    nz, ns = mesh.shape["rcv"], mesh.shape["src"]
    in_specs = (
        P(("freq", "src"), None, "rcv"),
        P(None, "freq", None),
        P(("freq", "rcv")),
        P(("freq", "rcv")),
        P(("freq", "rcv")),
        P(None, ("freq", "rcv"), "src"),
        P(("freq", "src"), None, "rcv"),
    )
    out_specs = P(("freq", "src"), None, "rcv")
    return jax.shard_map(
        functools.partial(per_device, nz, ns),
        mesh=mesh,
        in_specs=in_specs,
        out_specs=out_specs,
        check_vma=False,
    )
```

```python
import functools

import jax
import jax.numpy as jnp
from jax import lax
from jax.experimental import pallas as pl
from jax.experimental.pallas import tpu as pltpu
from jax.sharding import PartitionSpec as P

ITERS = 2
SUB = 8
LANES = 128
SOON = 4
SOONER = 4
LAG = 3
HOP = 1
BEHIND = 4
MESH = pl.DeviceIdType.MESH
F32 = jnp.float32
BF16 = jnp.bfloat16
NT = (((1,), (1,)), ((), ()))


def split(value):
    high = value.astype(BF16)
    return high, (value - high.astype(F32)).astype(BF16)


def remote(src, dst, send_sem, recv_sem, where):
    return pltpu.make_async_remote_copy(
        src_ref=src,
        dst_ref=dst,
        send_sem=send_sem,
        recv_sem=recv_sem,
        device_id=where,
        device_id_type=MESH,
    )


def kernel(
    nz, ns, groups, tables, fold, tile, steps,
    tr_ref, ow_ref, gr_ref, tb_ref, wt_ref, f_ref, a_ref, out_ref,
    codes, near, hot, picked, terms, found, sums, bins, order, b_own,
    a_all, pair, mine, give, take, pass_on, got, own, held, cols, acc,
    cs, cr, ts, tr, xs, xr, xl,
    a_sem, s1, r1, s2, r2, zs, zr, ps, pr, ls,
):
    z = lax.axis_index("rcv")
    c = lax.axis_index("src")
    core = lax.rem(c, 2)
    chip = c // 2
    chips = ns // 2
    shots, _, width = tr_ref.shape
    stencil = wt_ref.shape[0] // 2
    chunks = shots // SUB
    cells = nz * groups
    share = cells // ns
    outs = steps * tile
    early = steps // 2
    lag = LAG
    hop = HOP
    soon = SOON
    behind = BEHIND
    last = steps + lag - 1
    hs = shots // 2
    side = ns * hs
    sooner = min(SOONER, steps)

    def a_copy(t):
        rows = pl.ds(pl.multiple_of(t * tile, tile), tile)
        return pltpu.make_async_copy(a_ref.at[:, rows, :], a_all.at[:, rows, :], a_sem.at[t])

    for t in range(min(2, steps)):
        a_copy(t).start()

    def has(lane):
        other = z + 1 - 2 * lane
        return (other >= 0) & (other < nz)

    barrier = pltpu.get_barrier_semaphore()
    for lane in (0, 1):

        @pl.when(has(lane))
        def _():
            pl.semaphore_signal(
                barrier, inc=1, device_id={"rcv": z + 1 - 2 * lane}, device_id_type=MESH
            )

    for off in range(1, ns):
        pl.semaphore_signal(
            barrier, inc=1, device_id={"src": lax.rem(c + off, ns)}, device_id_type=MESH
        )
    codes[z, 0:1] = ow_ref[...]
    codes[z, 1:2] = gr_ref[...]
    codes[z, 2:3] = tb_ref[...]
    peers = jnp.where(z > 0, 1, 0) + jnp.where(z < nz - 1, 1, 0)
    pl.semaphore_wait(barrier, peers + ns - 1)

    def span(q):
        return pl.ds(pl.multiple_of(q * SUB, SUB), SUB)

    def raw(own, block, lane, dist, q):
        return remote(
            tr_ref.at[span(q)] if own else near.at[block, span(q)],
            near.at[block, span(q)],
            ts.at[lane, dist, q],
            tr.at[lane, dist, q],
            {"rcv": z + 1 - 2 * lane},
        )

    def code(block, lane, dist):
        return remote(
            codes.at[block],
            codes.at[block],
            cs.at[lane, dist],
            cr.at[lane, dist],
            {"rcv": z + 1 - 2 * lane},
        )

    w = wt_ref[...]
    w0 = w.astype(BF16)
    rest = w - w0.astype(F32)
    w1 = rest.astype(BF16)
    w2 = (rest - w1.astype(F32)).astype(BF16)
    table_ids = lax.broadcasted_iota(jnp.int32, (tables, width), 0)
    cell_ids = lax.broadcasted_iota(jnp.int32, (cells, width), 0)

    def prepare(block):
        cell = codes[block, 0:1] * groups + codes[block, 1:2]
        hot[block] = jnp.where(cell_ids == cell, 1.0, 0.0).astype(BF16)
        table_hot = jnp.where(table_ids == codes[block, 2:3], 1.0, 0.0).astype(BF16)
        picked[block] = sum(
            jnp.dot(part, table_hot, preferred_element_type=F32) for part in (w0, w1, w2)
        )

    def add_in(real, imag, block, start):
        for j in range(stencil):
            wr = picked[block, j : j + 1]
            wi = picked[block, stencil + j : stencil + j + 1]
            both = jnp.concatenate([real * wr - imag * wi, real * wi + imag * wr])
            top, rest = split(both)
            base = j * 4 * SUB
            terms[base : base + 2 * SUB, :] = top
            terms[base + 2 * SUB : base + 4 * SUB, :] = rest
        now = lax.dot_general(terms[...], hot[block], NT, preferred_element_type=F32)
        found[...] = now if start else found[...] + now

    def swap(q, who):
        return remote(sums.at[q, who], bins.at[q, c], xs.at[q, who], xr.at[q, c], {"src": who})

    def keep(q):
        return pltpu.make_async_copy(sums.at[q, c], bins.at[q, c], xl.at[q])

    def relay_in(q, dist):
        for lane in (0, 1):
            block = z - dist * (1 - 2 * lane)

            @pl.when((block >= 0) & (block < nz))
            def _():
                @pl.when(jnp.asarray(q == 0))
                def _():
                    code(block, lane, dist - 1).wait_recv()

                    @pl.when(has(lane))
                    def _():
                        code(block, lane, dist).start()

                raw(False, block, lane, dist - 1, q).wait_recv()

                @pl.when(has(lane))
                def _():
                    raw(False, block, lane, dist, q).start()

    def chunk(q, carry):
        @pl.when(q == 0)
        def _():
            for lane in (0, 1):

                @pl.when(has(lane))
                def _():
                    code(z, lane, 0).start()
                    raw(True, z, lane, 0, 0).start()

        @pl.when(q + 1 < chunks)
        def _():
            for lane in (0, 1):

                @pl.when(has(lane))
                def _():
                    raw(True, z, lane, 0, q + 1).start()

        @pl.when(q == 0)
        def _():
            prepare(z)

        add_in(tr_ref[span(q), 0, :], tr_ref[span(q), 1, :], z, True)

        def hop_in(dist, inner):
            @pl.when((q == 0) | (dist > 1))
            def _():
                relay_in(q, dist)

            @pl.when((dist == nz - 1) & (q + 1 < chunks))
            def _():
                relay_in(q + 1, 1)

            def add(lane, deeper):
                block = z - dist * (1 - 2 * lane)

                @pl.when((block >= 0) & (block < nz))
                def _():
                    @pl.when(q == 0)
                    def _():
                        prepare(block)

                    add_in(near[block, span(q), 0, :], near[block, span(q), 1, :], block, False)

                return deeper

            return lax.fori_loop(0, 2, add, inner)

        lax.fori_loop(1, nz, hop_in, 0)
        both = found[...].reshape(stencil, 2, 2 * SUB, cells)
        both = both[:, 0] + both[:, 1]
        for who in range(ns):
            sums[q, who] = both[:, :, who * share : (who + 1) * share]
        for off in range(ns - 1, 0, -1):
            swap(q, lax.rem(c + off, ns)).start()
        keep(q).start()
        return carry

    lax.fori_loop(0, chunks, chunk, 0)

    who = z // fold
    for j in range(stencil):
        rows = jnp.concatenate(
            [sums[q, who, j, p * SUB : (p + 1) * SUB] for p in (0, 1) for q in range(chunks)]
        )
        lanes = jnp.concatenate([rows] * (LANES // (2 * shots))).T
        order[0, pl.ds(j, share, stride=stencil), :] = lanes
    base = order[0, pl.ds(pl.multiple_of((z - who * fold) * outs, outs), outs), :]
    b_own[...] = base.T[: 2 * shots].reshape(2, shots, outs)

    def settle(h):
        first = h * chunks // 2

        def each(q, carry):
            keep(q).wait()
            for off in range(1, ns):
                peer = lax.rem(c + off, ns)
                remote(
                    bins.at[q, peer],
                    bins.at[q, peer],
                    xs.at[q, peer],
                    xr.at[q, peer],
                    {"src": peer},
                ).wait_recv()
            return carry

        lax.fori_loop(first, first + chunks // 2, each, 0)
        for j in range(stencil):
            rows = jnp.concatenate(
                [
                    bins[first + q, peer, j, p * SUB : (p + 1) * SUB]
                    for p in (0, 1)
                    for peer in range(ns)
                    for q in range(chunks // 2)
                ]
            )
            for g in range(2 * side // LANES):
                order[g, pl.ds(j, share, stride=stencil), :] = rows[g * LANES : (g + 1) * LANES].T
        for g in range(2 * side // LANES):
            top, rest = split(order[g].T)
            row = h * 2 * side + g * LANES
            pair[0, row : row + LANES, :] = top
            pair[1, row : row + LANES, :] = rest

    def to_partner(sweep, t):
        return remote(
            give.at[t],
            take.at[t],
            s1.at[sweep, t],
            r1.at[sweep, t],
            {"src": c + 1 - 2 * core},
        )

    def to_chip(sweep, t, off):
        who = 2 * lax.rem(chip + off, chips) + core
        return remote(
            pass_on.at[t, off - 1],
            got.at[t, off - 1],
            s2.at[sweep, t, off - 1],
            r2.at[sweep, t, off - 1],
            {"src": who},
        )

    def join(sums, row):
        return (
            sums[0][row : row + side] - sums[1][row + side : row + 2 * side],
            sums[1][row : row + side] + sums[0][row + side : row + 2 * side],
        )

    def times_half(h, t):
        rows = pl.ds(pl.multiple_of(t * tile, tile), tile)
        mine = pl.ds(pl.multiple_of(h * 2 * side, 2 * side), 2 * side)
        sums = []
        for part in (0, 1):
            top, rest = split(a_all[part, rows, :])
            now = lax.dot_general(
                pair[:, mine, :].reshape(4 * side, -1), top, NT, preferred_element_type=F32
            )
            now = now[: 2 * side] + now[2 * side :]
            now += lax.dot_general(pair[0, mine, :], rest, NT, preferred_element_type=F32)
            sums.append(now)
        return join(sums, 0)

    def times(t, ranges):
        rows = pl.ds(pl.multiple_of(t * tile, tile), tile)
        sums = []
        for part in (0, 1):
            total = None
            for cut in ranges:
                top, rest = split(a_all[part, rows, cut])
                now = lax.dot_general(pair[0, :, cut], top, NT, preferred_element_type=F32)
                now += lax.dot_general(pair[1, :, cut], top, NT, preferred_element_type=F32)
                now += lax.dot_general(pair[0, :, cut], rest, NT, preferred_element_type=F32)
                total = now if total is None else total + now
            sums.append(total)
        return join(sums, 0), join(sums, 2 * side)

    def fill(t, h, both):
        for part in (0, 1):
            for who in range(ns):
                value = both[part][who * hs : (who + 1) * hs]

                @pl.when(core == who % 2)
                def _():
                    mine[t, who // 2, part, h * hs : (h + 1) * hs] = value

                @pl.when(core != who % 2)
                def _():
                    give[t, who // 2, part, h * hs : (h + 1) * hs] = value

    def reduce_pair(sweep, t):
        to_partner(sweep, t).wait_recv()
        for off in range(1, chips):
            there = lax.rem(chip + off, chips)
            pass_on[t, off - 1] = mine[t, there] + take[t, there]
            to_chip(sweep, t, off).start()
        mine[t, chip] += take[t, chip]

    def finish(sweep, t):
        found = mine[t, chip]
        for off in range(1, chips):
            to_chip(sweep, t, off).wait_recv()
            found += got[t, off - 1]
        at = pl.ds(pl.multiple_of(t * tile, tile), tile)
        fr, fi = f_ref[:, 0, at], f_ref[:, 1, at]
        return (
            b_own[0, :, at] - (fr * found[0] - fi * found[1]),
            b_own[1, :, at] - (fr * found[1] + fi * found[0]),
        )

    def along(src, block, lane, dist, t):
        return remote(
            src,
            held.at[block, t],
            zs.at[lane, dist, t],
            zr.at[lane, dist, t],
            {"rcv": z + 1 - 2 * lane},
        )

    def across(src, block, t):
        f = block - (block // fold) * fold
        return remote(
            src, cols.at[f, t, c], ps.at[block, t], pr.at[c, f, t], {"src": block // fold}
        )

    def local(src, block, t):
        f = block - (block // fold) * fold
        return pltpu.make_async_copy(src, cols.at[f, t, c], ls.at[f, t])

    def hand_on(src, block, t):
        @pl.when(block // fold != c)
        def _():
            across(src, block, t).start()

        @pl.when(block // fold == c)
        def _():
            local(src, block, t).start()

    def relay(t, dist, fresh, give_it):
        for lane in (0, 1):
            block = z - dist * (1 - 2 * lane)

            @pl.when((block >= 0) & (block < nz))
            def _():
                @pl.when(jnp.asarray(fresh))
                def _():
                    along(held.at[block, t], block, lane, dist - 1, t).wait_recv()

                    @pl.when(has(lane))
                    def _():
                        along(held.at[block, t], block, lane, dist, t).start()

                @pl.when(jnp.asarray(give_it))
                def _():
                    hand_on(held.at[block, t], block, t)

    def first(step, carry):
        @pl.when(step < steps)
        def _():
            @pl.when(step < sooner)
            def _():
                fill(step, 1, times_half(1, step))

            @pl.when(step >= sooner)
            def _():
                a_copy(step).wait()

                @pl.when(step + 2 < steps)
                def _():
                    a_copy(step + 2).start()

                for h, both in enumerate(times(step, [pl.ds(0, fold * outs)])):
                    fill(step, h, both)

            to_partner(0, step).start()

        @pl.when((step >= 1) & (step <= steps))
        def _():
            reduce_pair(0, step - 1)

        @pl.when(step >= lag)
        def _():
            t = step - lag
            real, imag = finish(0, t)
            own[t, 0] = real
            own[t, 1] = imag
            for lane in (0, 1):

                @pl.when(has(lane))
                def _():
                    along(own.at[t], z, lane, 0, t).start()

            @pl.when(t < soon)
            def _():
                hand_on(own.at[t], z, t)

        def earlier(dist, inner):
            t = step - lag - hop * dist

            @pl.when(t >= 0)
            def _():
                relay(t, dist, True, t < soon)

            return inner

        return lax.fori_loop(1, nz, earlier, carry)

    def before(t, carry):
        a_copy(t).wait()

        @pl.when(t + 2 < steps)
        def _():
            a_copy(t + 2).start()

        fill(t, 0, times_half(0, t))
        return carry

    settle(0)
    lax.fori_loop(0, sooner, before, 0)
    settle(1)
    lax.fori_loop(0, last + 1, first, 0)

    def rest_of(t):
        @pl.when(t >= soon)
        def _():
            hand_on(own.at[t], z, t)

        def each(dist, carry):
            fresh = t + lag + hop * dist > last
            relay(t, dist, fresh, fresh | (t >= soon))
            return carry

        lax.fori_loop(1, nz, each, 0)

    def take_in(t, carry):
        for f in range(fold):
            local(own.at[t], c * fold + f, t).wait()
            for off in range(1, ns):
                who = lax.rem(c + off, ns)
                remote(
                    cols.at[f, t, who],
                    cols.at[f, t, who],
                    ps.at[0, t],
                    pr.at[who, f, t],
                    {"src": who},
                ).wait_recv()
            at = pl.ds(pl.multiple_of(f * outs + t * tile, tile), tile)
            for h in (0, 1):
                for part in (0, 1):
                    value = cols[f, t, :, part, h * hs : (h + 1) * hs]
                    top, rest = split(value.reshape(side, tile))
                    row = (2 * h + part) * side
                    pair[0, row : row + side, at] = top
                    pair[1, row : row + side, at] = rest
        return carry

    def range_of(start, size):
        return [pl.ds(f * outs + start * tile, size * tile) for f in range(fold)]

    for t in range(early):
        rest_of(t)
    lax.fori_loop(0, early, take_in, 0)
    share = -(-steps // (steps - early))

    def between(t, carry):
        rest_of(t)

        def some(i, inner):
            r = (t - early) * share + i

            @pl.when(r < steps)
            def _():
                for h, both in enumerate(times(r, range_of(0, early))):
                    acc[r, h, 0] = both[0]
                    acc[r, h, 1] = both[1]

            return inner

        return lax.fori_loop(0, share, some, carry)

    lax.fori_loop(early, steps, between, 0)
    lax.fori_loop(early, steps, take_in, 0)

    def sent(t, carry):
        to_partner(0, t).wait_send()
        for off in range(1, chips):
            to_chip(0, t, off).wait_send()
        return carry

    lax.fori_loop(0, steps, sent, 0)

    def second(step, carry):
        @pl.when(step < steps)
        def _():
            for h, both in enumerate(times(step, range_of(early, steps - early))):
                fill(step, h, (both[0] + acc[step, h, 0], both[1] + acc[step, h, 1]))
            to_partner(1, step).start()

        @pl.when((step >= 1) & (step <= steps))
        def _():
            reduce_pair(1, step - 1)

        @pl.when(step >= behind)
        def _():
            t = step - behind
            real, imag = finish(1, t)
            at = pl.ds(pl.multiple_of(t * tile, tile), tile)
            out_ref[:, 0, at] = real
            out_ref[:, 1, at] = imag

        return carry

    lax.fori_loop(0, steps + behind, second, 0)

    def drain(t, carry):
        to_partner(1, t).wait_send()
        for off in range(1, chips):
            to_chip(1, t, off).wait_send()

        def each(dist, inner):
            for lane in (0, 1):
                block = z - dist * (1 - 2 * lane)

                @pl.when((block >= 0) & (block < nz) & has(lane))
                def _():
                    along(held.at[block, t], block, lane, dist, t).wait_send()

            @pl.when(dist // fold != c)
            def _():
                across(held.at[dist, t], dist, t).wait_send()

            return inner

        return lax.fori_loop(0, nz, each, carry)

    lax.fori_loop(0, steps, drain, 0)

    def drain_in(q, carry):
        def each(dist, inner):
            for lane in (0, 1):
                block = z - dist * (1 - 2 * lane)

                @pl.when((block >= 0) & (block < nz) & has(lane))
                def _():
                    raw(False, block, lane, dist, q).wait_send()

                    @pl.when(q == 0)
                    def _():
                        code(block, lane, dist).wait_send()

            return inner

        for off in range(1, ns):
            swap(q, lax.rem(c + off, ns)).wait_send()
        return lax.fori_loop(0, nz, each, carry)

    lax.fori_loop(0, chunks, drain_in, 0)


def predict(traces, moveout, owner, group, table, aperture, shaping, nz, ns):
    tables, stencil = moveout.shape[1:]
    shots, _, width = traces.shape
    _, outs, depth = aperture.shape
    groups = outs // stencil
    fold = nz // ns
    chunks = shots // SUB
    cells = nz * groups
    share = cells // ns
    half = ns * shots
    tile = min(outs, 256)
    steps = outs // tile
    chips = ns // 2
    weights = jnp.transpose(moveout, (0, 2, 1)).reshape(2 * stencil, tables)
    dma = pltpu.SemaphoreType.DMA
    vmem = pl.BlockSpec(memory_space=pltpu.VMEM)
    part = (chunks, ns, stencil, 2 * SUB, share)
    block = (2, shots, tile)
    return pl.pallas_call(
        functools.partial(kernel, nz, ns, groups, tables, fold, tile, steps),
        out_shape=jax.ShapeDtypeStruct((shots, 2, outs), F32),
        in_specs=[vmem] * 6 + [pl.BlockSpec(memory_space=pl.ANY)],
        out_specs=vmem,
        scratch_shapes=[
            pltpu.VMEM((nz, 3, width), jnp.int32),
            pltpu.VMEM((nz, shots, 2, width), F32),
            pltpu.VMEM((nz, cells, width), BF16),
            pltpu.VMEM((nz, 2 * stencil, width), F32),
            pltpu.VMEM((stencil * 4 * SUB, width), BF16),
            pltpu.VMEM((stencil * 4 * SUB, cells), F32),
            pltpu.VMEM(part, F32),
            pltpu.VMEM(part, F32),
            pltpu.VMEM((half // LANES, share * stencil, LANES), F32),
            pltpu.VMEM((2, shots, outs), F32),
            pltpu.VMEM((2, outs, depth), F32),
            pltpu.VMEM((2, 2 * half, depth), BF16),
            pltpu.VMEM((steps, chips) + block, F32),
            pltpu.VMEM((steps, chips) + block, F32),
            pltpu.VMEM((steps, chips) + block, F32),
            pltpu.VMEM((steps, chips - 1) + block, F32),
            pltpu.VMEM((steps, chips - 1) + block, F32),
            pltpu.VMEM((steps,) + block, F32),
            pltpu.VMEM((nz, steps) + block, F32),
            pltpu.VMEM((fold, steps, ns) + block, F32),
            pltpu.VMEM((steps, 2, 2, half // 2, tile), F32),
            dma((2, nz)),
            dma((2, nz)),
            dma((2, nz, chunks)),
            dma((2, nz, chunks)),
            dma((chunks, ns)),
            dma((chunks, ns)),
            dma((chunks,)),
            dma((steps,)),
            dma((ITERS, steps)),
            dma((ITERS, steps)),
            dma((ITERS, steps, chips - 1)),
            dma((ITERS, steps, chips - 1)),
            dma((2, nz, steps)),
            dma((2, nz, steps)),
            dma((nz, steps)),
            dma((ns, fold, steps)),
            dma((fold, steps)),
        ],
        name="predict",
        compiler_params=pltpu.CompilerParams(
            collective_id=0, has_side_effects=True, vmem_limit_bytes=67043328
        ),
    )(traces, owner[None], group[None], table[None], weights, shaping, aperture)


def per_device(nz, ns, traces, moveout, owner, group, table, aperture, shaping):
    return predict(traces, moveout, owner, group, table, aperture, shaping, nz, ns)


def solution(mesh):
    nz, ns = mesh.shape["rcv"], mesh.shape["src"]
    in_specs = (
        P(("freq", "src"), None, "rcv"),
        P(None, "freq", None),
        P(("freq", "rcv")),
        P(("freq", "rcv")),
        P(("freq", "rcv")),
        P(None, ("freq", "rcv"), "src"),
        P(("freq", "src"), None, "rcv"),
    )
    out_specs = P(("freq", "src"), None, "rcv")
    return jax.shard_map(
        functools.partial(per_device, nz, ns),
        mesh=mesh,
        in_specs=in_specs,
        out_specs=out_specs,
        check_vma=False,
    )
```

```python
import functools

import jax
import jax.numpy as jnp
from jax import lax
from jax.experimental import pallas as pl
from jax.experimental.pallas import tpu as pltpu
from jax.sharding import PartitionSpec as P

ITERS = 2
SUB = 8
LANES = 128
SOON = 4
SOONER = 4
LAG = 3
HOP = 1
BEHIND = 4
MESH = pl.DeviceIdType.MESH
F32 = jnp.float32
BF16 = jnp.bfloat16
NT = (((1,), (1,)), ((), ()))


def split(value):
    high = value.astype(BF16)
    return high, (value - high.astype(F32)).astype(BF16)


def remote(src, dst, send_sem, recv_sem, where):
    return pltpu.make_async_remote_copy(
        src_ref=src,
        dst_ref=dst,
        send_sem=send_sem,
        recv_sem=recv_sem,
        device_id=where,
        device_id_type=MESH,
    )


def kernel(
    nz, ns, groups, tables, fold, tile, steps,
    tr_ref, ow_ref, gr_ref, tb_ref, wt_ref, f_ref, a_ref, out_ref,
    codes, near, hot, picked, terms, found, sums, bins, order, b_own,
    a_all, pair, mine, give, take, pass_on, got, own, held, cols, acc,
    cs, cr, ts, tr, xs, xr, xl,
    a_sem, s1, r1, s2, r2, zs, zr, ps, pr, ls,
):
    z = lax.axis_index("rcv")
    c = lax.axis_index("src")
    core = lax.rem(c, 2)
    chip = c // 2
    chips = ns // 2
    shots, _, width = tr_ref.shape
    stencil = wt_ref.shape[0] // 2
    chunks = shots // SUB
    cells = nz * groups
    share = cells // ns
    outs = steps * tile
    early = steps // 2
    lag = LAG
    hop = HOP
    soon = SOON
    behind = BEHIND
    last = steps + lag - 1
    hs = shots // 2
    side = ns * hs
    sooner = min(SOONER, steps)

    def a_copy(t):
        rows = pl.ds(pl.multiple_of(t * tile, tile), tile)
        return pltpu.make_async_copy(a_ref.at[:, rows, :], a_all.at[:, rows, :], a_sem.at[t])

    for t in range(min(2, steps)):
        a_copy(t).start()

    def has(lane):
        other = z + 1 - 2 * lane
        return (other >= 0) & (other < nz)

    barrier = pltpu.get_barrier_semaphore()
    for lane in (0, 1):

        @pl.when(has(lane))
        def _():
            pl.semaphore_signal(
                barrier, inc=1, device_id={"rcv": z + 1 - 2 * lane}, device_id_type=MESH
            )

    for off in range(1, ns):
        pl.semaphore_signal(
            barrier, inc=1, device_id={"src": lax.rem(c + off, ns)}, device_id_type=MESH
        )
    codes[z, 0:1] = ow_ref[...]
    codes[z, 1:2] = gr_ref[...]
    codes[z, 2:3] = tb_ref[...]
    peers = jnp.where(z > 0, 1, 0) + jnp.where(z < nz - 1, 1, 0)
    pl.semaphore_wait(barrier, peers + ns - 1)

    def span(q):
        return pl.ds(pl.multiple_of(q * SUB, SUB), SUB)

    def raw(own, block, lane, dist, q):
        return remote(
            tr_ref.at[span(q)] if own else near.at[block, span(q)],
            near.at[block, span(q)],
            ts.at[lane, dist, q],
            tr.at[lane, dist, q],
            {"rcv": z + 1 - 2 * lane},
        )

    def code(block, lane, dist):
        return remote(
            codes.at[block],
            codes.at[block],
            cs.at[lane, dist],
            cr.at[lane, dist],
            {"rcv": z + 1 - 2 * lane},
        )

    w = wt_ref[...]
    w0 = w.astype(BF16)
    rest = w - w0.astype(F32)
    w1 = rest.astype(BF16)
    w2 = (rest - w1.astype(F32)).astype(BF16)
    table_ids = lax.broadcasted_iota(jnp.int32, (tables, width), 0)
    cell_ids = lax.broadcasted_iota(jnp.int32, (cells, width), 0)

    def prepare(block):
        cell = codes[block, 0:1] * groups + codes[block, 1:2]
        hot[block] = jnp.where(cell_ids == cell, 1.0, 0.0).astype(BF16)
        table_hot = jnp.where(table_ids == codes[block, 2:3], 1.0, 0.0).astype(BF16)
        picked[block] = sum(
            jnp.dot(part, table_hot, preferred_element_type=F32) for part in (w0, w1, w2)
        )

    def add_in(real, imag, block, start):
        for j in range(stencil):
            wr = picked[block, j : j + 1]
            wi = picked[block, stencil + j : stencil + j + 1]
            both = jnp.concatenate([real * wr - imag * wi, real * wi + imag * wr])
            top, rest = split(both)
            base = j * 4 * SUB
            terms[base : base + 2 * SUB, :] = top
            terms[base + 2 * SUB : base + 4 * SUB, :] = rest
        now = lax.dot_general(terms[...], hot[block], NT, preferred_element_type=F32)
        found[...] = now if start else found[...] + now

    def swap(q, who):
        return remote(sums.at[q, who], bins.at[q, c], xs.at[q, who], xr.at[q, c], {"src": who})

    def keep(q):
        return pltpu.make_async_copy(sums.at[q, c], bins.at[q, c], xl.at[q])

    def relay_in(q, dist):
        for lane in (0, 1):
            block = z - dist * (1 - 2 * lane)

            @pl.when((block >= 0) & (block < nz))
            def _():
                @pl.when(jnp.asarray(q == 0))
                def _():
                    code(block, lane, dist - 1).wait_recv()

                    @pl.when(has(lane))
                    def _():
                        code(block, lane, dist).start()

                    prepare(block)

                raw(False, block, lane, dist - 1, q).wait_recv()

                @pl.when(has(lane))
                def _():
                    raw(False, block, lane, dist, q).start()

    def chunk(q, carry):
        @pl.when(q == 0)
        def _():
            for lane in (0, 1):

                @pl.when(has(lane))
                def _():
                    code(z, lane, 0).start()
                    raw(True, z, lane, 0, 0).start()

        @pl.when(q + 1 < chunks)
        def _():
            for lane in (0, 1):

                @pl.when(has(lane))
                def _():
                    raw(True, z, lane, 0, q + 1).start()

        @pl.when(q == 0)
        def _():
            prepare(z)

        add_in(tr_ref[span(q), 0, :], tr_ref[span(q), 1, :], z, True)

        def hop_in(dist, inner):
            @pl.when((q == 0) | (dist > 1))
            def _():
                relay_in(q, dist)

            @pl.when((dist == nz - 1) & (q + 1 < chunks))
            def _():
                relay_in(q + 1, 1)

            def add(lane, deeper):
                block = z - dist * (1 - 2 * lane)

                @pl.when((block >= 0) & (block < nz))
                def _():
                    add_in(near[block, span(q), 0, :], near[block, span(q), 1, :], block, False)

                return deeper

            return lax.fori_loop(0, 2, add, inner)

        lax.fori_loop(1, nz, hop_in, 0)
        both = found[...].reshape(stencil, 2, 2 * SUB, cells)
        both = both[:, 0] + both[:, 1]
        for who in range(ns):
            sums[q, who] = both[:, :, who * share : (who + 1) * share]
        for off in range(ns - 1, 0, -1):
            swap(q, lax.rem(c + off, ns)).start()
        keep(q).start()
        return carry

    lax.fori_loop(0, chunks, chunk, 0)

    who = z // fold
    for j in range(stencil):
        rows = jnp.concatenate(
            [sums[q, who, j, p * SUB : (p + 1) * SUB] for p in (0, 1) for q in range(chunks)]
        )
        lanes = jnp.concatenate([rows] * (LANES // (2 * shots))).T
        order[0, pl.ds(j, share, stride=stencil), :] = lanes
    base = order[0, pl.ds(pl.multiple_of((z - who * fold) * outs, outs), outs), :]
    b_own[...] = base.T[: 2 * shots].reshape(2, shots, outs)

    def settle(h):
        first = h * chunks // 2

        def each(q, carry):
            keep(q).wait()
            for off in range(1, ns):
                peer = lax.rem(c + off, ns)
                remote(
                    bins.at[q, peer],
                    bins.at[q, peer],
                    xs.at[q, peer],
                    xr.at[q, peer],
                    {"src": peer},
                ).wait_recv()
            return carry

        lax.fori_loop(first, first + chunks // 2, each, 0)
        for j in range(stencil):
            rows = jnp.concatenate(
                [
                    bins[first + q, peer, j, p * SUB : (p + 1) * SUB]
                    for p in (0, 1)
                    for peer in range(ns)
                    for q in range(chunks // 2)
                ]
            )
            for g in range(2 * side // LANES):
                order[g, pl.ds(j, share, stride=stencil), :] = rows[g * LANES : (g + 1) * LANES].T
        for g in range(2 * side // LANES):
            top, rest = split(order[g].T)
            row = h * 2 * side + g * LANES
            pair[0, row : row + LANES, :] = top
            pair[1, row : row + LANES, :] = rest

    def to_partner(sweep, t):
        return remote(
            give.at[t],
            take.at[t],
            s1.at[sweep, t],
            r1.at[sweep, t],
            {"src": c + 1 - 2 * core},
        )

    def to_chip(sweep, t, off):
        who = 2 * lax.rem(chip + off, chips) + core
        return remote(
            pass_on.at[t, off - 1],
            got.at[t, off - 1],
            s2.at[sweep, t, off - 1],
            r2.at[sweep, t, off - 1],
            {"src": who},
        )

    def join(sums, row):
        return (
            sums[0][row : row + side] - sums[1][row + side : row + 2 * side],
            sums[1][row : row + side] + sums[0][row + side : row + 2 * side],
        )

    def times_half(h, t):
        rows = pl.ds(pl.multiple_of(t * tile, tile), tile)
        mine = pl.ds(pl.multiple_of(h * 2 * side, 2 * side), 2 * side)
        sums = []
        for part in (0, 1):
            top, rest = split(a_all[part, rows, :])
            now = lax.dot_general(
                pair[:, mine, :].reshape(4 * side, -1), top, NT, preferred_element_type=F32
            )
            now = now[: 2 * side] + now[2 * side :]
            now += lax.dot_general(pair[0, mine, :], rest, NT, preferred_element_type=F32)
            sums.append(now)
        return join(sums, 0)

    def times(t, ranges):
        rows = pl.ds(pl.multiple_of(t * tile, tile), tile)
        sums = []
        for part in (0, 1):
            total = None
            for cut in ranges:
                top, rest = split(a_all[part, rows, cut])
                now = lax.dot_general(pair[0, :, cut], top, NT, preferred_element_type=F32)
                now += lax.dot_general(pair[1, :, cut], top, NT, preferred_element_type=F32)
                now += lax.dot_general(pair[0, :, cut], rest, NT, preferred_element_type=F32)
                total = now if total is None else total + now
            sums.append(total)
        return join(sums, 0), join(sums, 2 * side)

    def fill(t, h, both):
        for part in (0, 1):
            for who in range(ns):
                value = both[part][who * hs : (who + 1) * hs]

                @pl.when(core == who % 2)
                def _():
                    mine[t, who // 2, part, h * hs : (h + 1) * hs] = value

                @pl.when(core != who % 2)
                def _():
                    give[t, who // 2, part, h * hs : (h + 1) * hs] = value

    def reduce_pair(sweep, t):
        to_partner(sweep, t).wait_recv()
        for off in range(1, chips):
            there = lax.rem(chip + off, chips)
            pass_on[t, off - 1] = mine[t, there] + take[t, there]
            to_chip(sweep, t, off).start()
        mine[t, chip] += take[t, chip]

    def finish(sweep, t):
        found = mine[t, chip]
        for off in range(1, chips):
            to_chip(sweep, t, off).wait_recv()
            found += got[t, off - 1]
        at = pl.ds(pl.multiple_of(t * tile, tile), tile)
        fr, fi = f_ref[:, 0, at], f_ref[:, 1, at]
        return (
            b_own[0, :, at] - (fr * found[0] - fi * found[1]),
            b_own[1, :, at] - (fr * found[1] + fi * found[0]),
        )

    def along(src, block, lane, dist, t):
        return remote(
            src,
            held.at[block, t],
            zs.at[lane, dist, t],
            zr.at[lane, dist, t],
            {"rcv": z + 1 - 2 * lane},
        )

    def across(src, block, t):
        f = block - (block // fold) * fold
        return remote(
            src, cols.at[f, t, c], ps.at[block, t], pr.at[c, f, t], {"src": block // fold}
        )

    def local(src, block, t):
        f = block - (block // fold) * fold
        return pltpu.make_async_copy(src, cols.at[f, t, c], ls.at[f, t])

    def hand_on(src, block, t):
        @pl.when(block // fold != c)
        def _():
            across(src, block, t).start()

        @pl.when(block // fold == c)
        def _():
            local(src, block, t).start()

    def relay(t, dist, fresh, give_it):
        for lane in (0, 1):
            block = z - dist * (1 - 2 * lane)

            @pl.when((block >= 0) & (block < nz))
            def _():
                @pl.when(jnp.asarray(fresh))
                def _():
                    along(held.at[block, t], block, lane, dist - 1, t).wait_recv()

                    @pl.when(has(lane))
                    def _():
                        along(held.at[block, t], block, lane, dist, t).start()

                @pl.when(jnp.asarray(give_it))
                def _():
                    hand_on(held.at[block, t], block, t)

    def first(step, carry):
        @pl.when(step < steps)
        def _():
            @pl.when(step < sooner)
            def _():
                fill(step, 1, times_half(1, step))

            @pl.when(step >= sooner)
            def _():
                a_copy(step).wait()

                @pl.when(step + 2 < steps)
                def _():
                    a_copy(step + 2).start()

                for h, both in enumerate(times(step, [pl.ds(0, fold * outs)])):
                    fill(step, h, both)

            to_partner(0, step).start()

        @pl.when((step >= 1) & (step <= steps))
        def _():
            reduce_pair(0, step - 1)

        @pl.when(step >= lag)
        def _():
            t = step - lag
            real, imag = finish(0, t)
            own[t, 0] = real
            own[t, 1] = imag
            for lane in (0, 1):

                @pl.when(has(lane))
                def _():
                    along(own.at[t], z, lane, 0, t).start()

            @pl.when(t < soon)
            def _():
                hand_on(own.at[t], z, t)

        def earlier(dist, inner):
            t = step - lag - hop * dist

            @pl.when(t >= 0)
            def _():
                relay(t, dist, True, t < soon)

            return inner

        return lax.fori_loop(1, nz, earlier, carry)

    def before(t, carry):
        a_copy(t).wait()

        @pl.when(t + 2 < steps)
        def _():
            a_copy(t + 2).start()

        fill(t, 0, times_half(0, t))
        return carry

    settle(0)
    lax.fori_loop(0, sooner, before, 0)
    settle(1)
    lax.fori_loop(0, last + 1, first, 0)

    def rest_of(t):
        @pl.when(t >= soon)
        def _():
            hand_on(own.at[t], z, t)

        def each(dist, carry):
            fresh = t + lag + hop * dist > last
            relay(t, dist, fresh, fresh | (t >= soon))
            return carry

        lax.fori_loop(1, nz, each, 0)

    def take_in(t, carry):
        for f in range(fold):
            local(own.at[t], c * fold + f, t).wait()
            for off in range(1, ns):
                who = lax.rem(c + off, ns)
                remote(
                    cols.at[f, t, who],
                    cols.at[f, t, who],
                    ps.at[0, t],
                    pr.at[who, f, t],
                    {"src": who},
                ).wait_recv()
            at = pl.ds(pl.multiple_of(f * outs + t * tile, tile), tile)
            for h in (0, 1):
                for part in (0, 1):
                    value = cols[f, t, :, part, h * hs : (h + 1) * hs]
                    top, rest = split(value.reshape(side, tile))
                    row = (2 * h + part) * side
                    pair[0, row : row + side, at] = top
                    pair[1, row : row + side, at] = rest
        return carry

    def range_of(start, size):
        return [pl.ds(f * outs + start * tile, size * tile) for f in range(fold)]

    for t in range(early):
        rest_of(t)
    lax.fori_loop(0, early, take_in, 0)
    share = -(-steps // (steps - early))

    def between(t, carry):
        rest_of(t)

        def some(i, inner):
            r = (t - early) * share + i

            @pl.when(r < steps)
            def _():
                for h, both in enumerate(times(r, range_of(0, early))):
                    acc[r, h, 0] = both[0]
                    acc[r, h, 1] = both[1]

            return inner

        return lax.fori_loop(0, share, some, carry)

    lax.fori_loop(early, steps, between, 0)
    lax.fori_loop(early, steps, take_in, 0)

    def sent(t, carry):
        to_partner(0, t).wait_send()
        for off in range(1, chips):
            to_chip(0, t, off).wait_send()
        return carry

    lax.fori_loop(0, steps, sent, 0)

    def second(step, carry):
        @pl.when(step < steps)
        def _():
            for h, both in enumerate(times(step, range_of(early, steps - early))):
                fill(step, h, (both[0] + acc[step, h, 0], both[1] + acc[step, h, 1]))
            to_partner(1, step).start()

        @pl.when((step >= 1) & (step <= steps))
        def _():
            reduce_pair(1, step - 1)

        @pl.when(step >= behind)
        def _():
            t = step - behind
            real, imag = finish(1, t)
            at = pl.ds(pl.multiple_of(t * tile, tile), tile)
            out_ref[:, 0, at] = real
            out_ref[:, 1, at] = imag

        return carry

    lax.fori_loop(0, steps + behind, second, 0)

    def drain(t, carry):
        to_partner(1, t).wait_send()
        for off in range(1, chips):
            to_chip(1, t, off).wait_send()

        def each(dist, inner):
            for lane in (0, 1):
                block = z - dist * (1 - 2 * lane)

                @pl.when((block >= 0) & (block < nz) & has(lane))
                def _():
                    along(held.at[block, t], block, lane, dist, t).wait_send()

            @pl.when(dist // fold != c)
            def _():
                across(held.at[dist, t], dist, t).wait_send()

            return inner

        return lax.fori_loop(0, nz, each, carry)

    lax.fori_loop(0, steps, drain, 0)

    def drain_in(q, carry):
        def each(dist, inner):
            for lane in (0, 1):
                block = z - dist * (1 - 2 * lane)

                @pl.when((block >= 0) & (block < nz) & has(lane))
                def _():
                    raw(False, block, lane, dist, q).wait_send()

                    @pl.when(q == 0)
                    def _():
                        code(block, lane, dist).wait_send()

            return inner

        for off in range(1, ns):
            swap(q, lax.rem(c + off, ns)).wait_send()
        return lax.fori_loop(0, nz, each, carry)

    lax.fori_loop(0, chunks, drain_in, 0)


def predict(traces, moveout, owner, group, table, aperture, shaping, nz, ns):
    tables, stencil = moveout.shape[1:]
    shots, _, width = traces.shape
    _, outs, depth = aperture.shape
    groups = outs // stencil
    fold = nz // ns
    chunks = shots // SUB
    cells = nz * groups
    share = cells // ns
    half = ns * shots
    tile = min(outs, 256)
    steps = outs // tile
    chips = ns // 2
    weights = jnp.transpose(moveout, (0, 2, 1)).reshape(2 * stencil, tables)
    dma = pltpu.SemaphoreType.DMA
    vmem = pl.BlockSpec(memory_space=pltpu.VMEM)
    part = (chunks, ns, stencil, 2 * SUB, share)
    block = (2, shots, tile)
    return pl.pallas_call(
        functools.partial(kernel, nz, ns, groups, tables, fold, tile, steps),
        out_shape=jax.ShapeDtypeStruct((shots, 2, outs), F32),
        in_specs=[vmem] * 6 + [pl.BlockSpec(memory_space=pl.ANY)],
        out_specs=vmem,
        scratch_shapes=[
            pltpu.VMEM((nz, 3, width), jnp.int32),
            pltpu.VMEM((nz, shots, 2, width), F32),
            pltpu.VMEM((nz, cells, width), BF16),
            pltpu.VMEM((nz, 2 * stencil, width), F32),
            pltpu.VMEM((stencil * 4 * SUB, width), BF16),
            pltpu.VMEM((stencil * 4 * SUB, cells), F32),
            pltpu.VMEM(part, F32),
            pltpu.VMEM(part, F32),
            pltpu.VMEM((half // LANES, share * stencil, LANES), F32),
            pltpu.VMEM((2, shots, outs), F32),
            pltpu.VMEM((2, outs, depth), F32),
            pltpu.VMEM((2, 2 * half, depth), BF16),
            pltpu.VMEM((steps, chips) + block, F32),
            pltpu.VMEM((steps, chips) + block, F32),
            pltpu.VMEM((steps, chips) + block, F32),
            pltpu.VMEM((steps, chips - 1) + block, F32),
            pltpu.VMEM((steps, chips - 1) + block, F32),
            pltpu.VMEM((steps,) + block, F32),
            pltpu.VMEM((nz, steps) + block, F32),
            pltpu.VMEM((fold, steps, ns) + block, F32),
            pltpu.VMEM((steps, 2, 2, half // 2, tile), F32),
            dma((2, nz)),
            dma((2, nz)),
            dma((2, nz, chunks)),
            dma((2, nz, chunks)),
            dma((chunks, ns)),
            dma((chunks, ns)),
            dma((chunks,)),
            dma((steps,)),
            dma((ITERS, steps)),
            dma((ITERS, steps)),
            dma((ITERS, steps, chips - 1)),
            dma((ITERS, steps, chips - 1)),
            dma((2, nz, steps)),
            dma((2, nz, steps)),
            dma((nz, steps)),
            dma((ns, fold, steps)),
            dma((fold, steps)),
        ],
        name="predict",
        compiler_params=pltpu.CompilerParams(
            collective_id=0, has_side_effects=True, vmem_limit_bytes=67043328
        ),
    )(traces, owner[None], group[None], table[None], weights, shaping, aperture)


def per_device(nz, ns, traces, moveout, owner, group, table, aperture, shaping):
    return predict(traces, moveout, owner, group, table, aperture, shaping, nz, ns)


def solution(mesh):
    nz, ns = mesh.shape["rcv"], mesh.shape["src"]
    in_specs = (
        P(("freq", "src"), None, "rcv"),
        P(None, "freq", None),
        P(("freq", "rcv")),
        P(("freq", "rcv")),
        P(("freq", "rcv")),
        P(None, ("freq", "rcv"), "src"),
        P(("freq", "src"), None, "rcv"),
    )
    out_specs = P(("freq", "src"), None, "rcv")
    return jax.shard_map(
        functools.partial(per_device, nz, ns),
        mesh=mesh,
        in_specs=in_specs,
        out_specs=out_specs,
        check_vma=False,
    )
```
